128 devices in a mesh: ctx: 8 (over x, z_hi), frame: 16 (over z_lo, y, core).
Axes of the slice: x: 4, y: 4, z: 4 (z_hi: 2, z_lo: 2; z = z_hi * 2 + z_lo), core: 2. Of those that a mesh axis runs over, the one named last changes fastest.
Arguments:
- queries: bfloat16 [4096, 4096], P('ctx', 'frame'), may hold values from -160 to 160
- keys: bfloat16 [8192, 4096], P('ctx', 'frame'), may hold values from -4 to 4
- values: bfloat16 [8192, 4096], P('ctx', 'frame'), may hold values from -6 to 6
- query_frames: int32 [256], P('ctx'), may hold values from 0 to 383, as said below
- frame_counts: int32 [512], replicated, may hold values from 0 to 16, as said below
- clip_of_frame: int32 [256], P('ctx'), may hold values from 0 to 15, as said below
- in_proj: bfloat16 [4096, 1024], P('frame'), may hold values from -0.09375 to 0.09375
- mlp_up: bfloat16 [1024, 4096], replicated, may hold values from -0.1875 to 0.1875
- mlp_down: bfloat16 [4096, 1024], replicated, may hold values from -0.09375 to 0.09375
- reward_head: float32 [1024], replicated, may hold values from -0.1875 to 0.1875
Outputs:
- query_grad: float32 [4096, 4096], P('ctx', 'frame')
- key_grad: float32 [8192, 4096], P('ctx', 'frame')
- value_grad: float32 [8192, 4096], P('ctx', 'frame')
- clip_reward: float32 [128], P(('ctx', 'frame'))
The draws below stay inside these ranges and needn't reach their ends.
Inputs may be any that keep to these rules, and one draw needn't show every extreme that they name: `query_frames`: the query patch rows are distinct rows of the first 512 * 3 // 4 patch rows of the video, in increasing order, all of them live; the first and the last of those rows are always among them. `frame_counts`: the live tokens are a prefix of the sequence of at least three quarters of it: rows before the prefix's end are full, one row may be partly live, the rows after it have none, and the last row has none. `clip_of_frame`: within each aligned block of 32 patch row slots every clip number appears exactly 2 times.
All inputs are finite; a program needn't handle non-finite values.
Results may differ from the reference program's by a relative error of at most 0.02.
Values may be sent and summed in bfloat16 or wider, within the bound.
No kernel may reach another device: no remote copies, remote signals or barrier semaphores. Data moves between devices by JAX's collectives and lax.ppermute only.
A program may use at most 192 MiB of HBM per device.

```python
import math
import jax
import jax.numpy as jnp
from jax import lax

HD = 128
VD = 1024
VFF = 4096
FTOK = 16
CLIP = 2
HEADS = 32
D = 4096
KTOK = 8192
KFRAMES = 512
QFR_DEV = 32
QTOK = 4096
QFRAMES = 256
NCLIPS = 128
N_FRAME = 16


def draw_keys(key, part):
    return jax.random.truncated_normal(jax.random.fold_in(key, 5), -4.0, 4.0, (KTOK, D), jnp.float32).astype(jnp.bfloat16)


def draw_query_frames(key, part):
    range_rows = KFRAMES * 3 // 4
    order = jax.random.permutation(jax.random.fold_in(key, 41), range_rows - 2)[:QFRAMES - 2] + 1
    inner = jnp.sort(order.astype(jnp.int32))
    first = jnp.zeros((1,), jnp.int32)
    last = jnp.full((1,), range_rows - 1, jnp.int32)
    return jnp.concatenate([first, inner, last]).astype(jnp.int32)


def draw_queries(key, part):
    base_key = jax.random.fold_in(jax.random.fold_in(key, 11), 0)
    base_draw = jax.random.truncated_normal(base_key, -4.0, 4.0, (QTOK, D), jnp.float32)
    result = base_draw
    return result.astype(jnp.bfloat16)


def layout_length(key):
    return jax.random.randint(jax.random.fold_in(key, 37), (), KTOK * 3 // 4, KTOK - FTOK + 1)


def draw_frame_counts(key, part):
    live_length = layout_length(key)
    remain = live_length - jnp.arange(KFRAMES, dtype=jnp.int32) * FTOK
    return jnp.clip(remain, 0, FTOK).astype(jnp.int32)


def draw_clip_of_frame(key, part):
    block_count = QFRAMES // QFR_DEV
    block_keys = jax.random.split(jax.random.fold_in(key, 23), block_count)

    def one_block(block_key):
        return jax.random.permutation(block_key, QFR_DEV)
    orders = jax.vmap(one_block)(block_keys)
    return (orders // CLIP).reshape(-1).astype(jnp.int32)


def levels(key, extent, shards, low, high):
    loudness = 1.0
    for axis_at, blocks in shards:
        steps = jax.random.uniform(jax.random.fold_in(jax.random.fold_in(key, 6), axis_at), (blocks,), jnp.float32, low / len(shards), high / len(shards))
        loudness = loudness * jnp.repeat(jnp.exp(steps), extent[axis_at] // blocks).reshape((-1,) + (1,) * (len(extent) - 1 - axis_at))
    return loudness


def centred(rng, dims, scale, reach, shards=(), kind=jnp.bfloat16):
    loudness = levels(rng, dims, shards, -0.22, 0.18) if shards else 1.0
    values = jax.random.normal(rng, dims, jnp.float32) * scale * loudness
    return jnp.minimum(jnp.maximum(values, -reach), reach).astype(kind)


def setup_inputs(seed: int = 0) -> dict:
    key_of = jax.random.split(jax.random.key(seed), 11)
    queries = draw_queries(jax.random.fold_in(key_of[10], 71), 0)
    keys = draw_keys(jax.random.fold_in(key_of[10], 71), 0)
    values = centred(key_of[2], (KTOK, D), 1.0, 6.0, ((0, 8), (1, 16)))
    query_frames = draw_query_frames(jax.random.fold_in(key_of[10], 71), 0)
    frame_counts = draw_frame_counts(jax.random.fold_in(key_of[10], 71), 0)
    clip_of_frame = draw_clip_of_frame(jax.random.fold_in(key_of[10], 71), 0)
    in_proj = centred(key_of[6], (D, VD), D ** -0.5, 0.09375, ((0, 16),))
    mlp_up = centred(key_of[7], (VD, VFF), VD ** -0.5, 0.1875)
    mlp_down = centred(key_of[8], (VFF, VD), VFF ** -0.5, 0.09375)
    reward_head = centred(key_of[9], (VD,), VD ** -0.5, 0.1875, (), jnp.float32)
    return {"queries": queries, "keys": keys, "values": values, "query_frames": query_frames, "frame_counts": frame_counts, "clip_of_frame": clip_of_frame, "in_proj": in_proj, "mlp_up": mlp_up, "mlp_down": mlp_down, "reward_head": reward_head}


EPSILON = 1e-05

def rotate(values_in, position, inverse):
    row_count = values_in.shape[0]
    half_width = HD // 2
    pieces = values_in.reshape(row_count, -1, HD)
    frequency = jnp.exp(-math.log(10000.0) * jnp.arange(half_width, dtype=jnp.float32) / half_width)
    angle = position.astype(jnp.float32)[:, None] * frequency[None, :]
    cosine = jnp.cos(angle)[:, None, :]
    sine = jnp.sin(angle)[:, None, :]
    if inverse:
        sine = -sine
    first_half = pieces[:, :, :half_width]
    second_half = pieces[:, :, half_width:]
    result = jnp.concatenate([first_half * cosine - second_half * sine, second_half * cosine + first_half * sine], axis=2)
    return result.reshape(row_count, -1)

def normalize(values_in):
    center = lax.optimization_barrier(jnp.mean(values_in, axis=-1, keepdims=True))
    centered = values_in - center
    variance = lax.optimization_barrier(jnp.mean(centered * centered, axis=-1, keepdims=True))
    return centered * lax.rsqrt(variance + EPSILON)

def head_scores(query_head, key_head, key_valid):
    scores = jnp.dot(query_head, key_head.T, preferred_element_type=jnp.float32) * (1.0 / math.sqrt(HD))
    return jnp.where(key_valid[None, :], scores, -jnp.inf)

def head_forward(operand, key_valid):
    query_head, key_head, value_head = operand
    scores = head_scores(query_head, key_head, key_valid)
    largest = lax.optimization_barrier(jnp.max(scores, axis=1))
    total = lax.optimization_barrier(jnp.sum(jnp.exp(scores - largest[:, None]), axis=1))
    log_total = largest + jnp.log(total)
    weights = jnp.exp(scores - log_total[:, None])
    output = jnp.dot(weights.astype(jnp.bfloat16), value_head, preferred_element_type=jnp.float32).astype(jnp.bfloat16)
    return (output, log_total)

def head_backward(operand, key_valid):
    query_head, key_head, value_head, out_head, grad_head, log_total = operand
    scores = head_scores(query_head, key_head, key_valid)
    weights = jnp.exp(scores - log_total[:, None])
    weights_low = weights.astype(jnp.bfloat16)
    delta = lax.optimization_barrier(jnp.sum(grad_head.astype(jnp.float32) * out_head.astype(jnp.float32), axis=1))
    value_grad = jnp.dot(weights_low.T, grad_head, preferred_element_type=jnp.float32)
    weight_grad = jnp.dot(grad_head, value_head.T, preferred_element_type=jnp.float32)
    score_grad = (weights * (weight_grad - delta[:, None]) * (1.0 / math.sqrt(HD))).astype(jnp.bfloat16)
    query_grad = jnp.dot(score_grad, key_head, preferred_element_type=jnp.float32)
    key_grad = jnp.dot(score_grad.T, query_head, preferred_element_type=jnp.float32)
    return (query_grad, key_grad, value_grad)

def split_heads(array):
    return array.reshape(array.shape[0], HEADS, HD).transpose(1, 0, 2)

def join_heads(array):
    return array.transpose(1, 0, 2).reshape(array.shape[1], HEADS * HD)

def reference(queries, keys, values, query_frames, frame_counts, clip_of_frame, in_proj, mlp_up, mlp_down, reward_head):
    in_frame = jnp.arange(FTOK, dtype=jnp.int32)
    query_position = (query_frames[:, None] * FTOK + in_frame[None, :]).reshape(-1)
    key_position = jnp.arange(KTOK, dtype=jnp.int32)
    key_valid = (in_frame[None, :] < frame_counts[:, None]).reshape(-1)
    slot_counts = frame_counts[query_frames]
    query_valid = (in_frame[None, :] < slot_counts[:, None]).reshape(-1)
    slot_index = jnp.arange(QFRAMES, dtype=jnp.int32)
    slot_clip = slot_index // QFR_DEV * N_FRAME + clip_of_frame
    row_clip = jnp.repeat(slot_clip, FTOK)
    rotated_query = rotate(queries.astype(jnp.float32), query_position, False).astype(jnp.bfloat16)
    rotated_key = rotate(keys.astype(jnp.float32), key_position, False).astype(jnp.bfloat16)
    query_heads = split_heads(rotated_query)
    key_heads = split_heads(rotated_key)
    value_heads = split_heads(values)
    out_heads, log_totals = lax.map(partial_forward(key_valid), (query_heads, key_heads, value_heads))
    attention_out = join_heads(out_heads)
    clip_inputs = jnp.dot(attention_out, in_proj, preferred_element_type=jnp.float32)

    def score_clips(inputs):
        normed = normalize(inputs).astype(jnp.bfloat16)
        expanded = jax.nn.gelu(jnp.dot(normed, mlp_up, preferred_element_type=jnp.float32)).astype(jnp.bfloat16)
        hidden = jnp.dot(expanded, mlp_down, preferred_element_type=jnp.float32)
        live = query_valid.astype(jnp.float32)
        sums = jax.ops.segment_sum(hidden * live[:, None], row_clip, NCLIPS)
        counts = jax.ops.segment_sum(live, row_clip, NCLIPS)
        pooled = sums / counts[:, None]
        return counts * jnp.dot(normalize(pooled), reward_head, precision=lax.Precision.HIGHEST)
    rewards, pull_back = jax.vjp(score_clips, clip_inputs)
    input_grad, = pull_back(jnp.ones_like(rewards))
    out_grad = jnp.dot(input_grad.astype(jnp.bfloat16), in_proj.T, preferred_element_type=jnp.float32).astype(jnp.bfloat16)
    query_grad, key_grad, value_grad = lax.map(partial_backward(key_valid), (query_heads, key_heads, value_heads, out_heads, split_heads(out_grad), log_totals))
    query_result = rotate(join_heads(query_grad), query_position, True)
    key_result = rotate(join_heads(key_grad), key_position, True)
    return (query_result, key_result, join_heads(value_grad), rewards)

def partial_forward(key_valid):

    def apply_head(operand):
        return head_forward(operand, key_valid)
    return apply_head

def partial_backward(key_valid):

    def apply_head(operand):
        return head_backward(operand, key_valid)
    return apply_head
```

```python
import functools
import math

import jax
import jax.numpy as jnp
from jax import lax
from jax.experimental import pallas as pl
from jax.experimental.pallas import tpu as pltpu
from jax.sharding import PartitionSpec as P

HD = 128
FTOK = 16
CLIP = 2
EPSILON = 1e-05
SCALE = 1.0 / math.sqrt(HD)
EXP2_SCALE = SCALE * math.log2(math.e)
DEAD = -1e30
EXTRA = 16
CHUNK = 512


f32 = jnp.float32
bf16 = jnp.bfloat16

NN = (((1,), (0,)), ((), ()))
NT = (((1,), (1,)), ((), ()))
TN = (((0,), (0,)), ((), ()))

VMEM = pl.BlockSpec(memory_space=pltpu.VMEM)
SMEM = pl.BlockSpec(memory_space=pltpu.SMEM)


def dot(left, right, dims):
    return lax.dot_general(left, right, dims, preferred_element_type=f32)


def call(kernel, in_specs, outs, scratch=()):
    return pl.pallas_call(
        kernel,
        out_shape=[jax.ShapeDtypeStruct(shape, dtype) for shape, dtype in outs],
        in_specs=in_specs,
        out_specs=[VMEM] * len(outs),
        scratch_shapes=list(scratch),
        compiler_params=pltpu.CompilerParams(vmem_limit_bytes=56 * 1024 * 1024),
    )


def split3(x):
    high = x.astype(bf16).astype(f32)
    rest = x - high
    middle = rest.astype(bf16).astype(f32)
    low = (rest - middle).astype(bf16).astype(f32)
    return high, middle, low


def rotate_kernel(at, q, k, v, cq, sq, ck, sk, qs, qo, ks, ko, vs, vo):
    z = at[0]

    def rot(x, c, s):
        x = x.astype(f32)
        return x * c + pltpu.roll(x, HD // 2, 1) * s

    for which in range(2):

        @pl.when(z == which)
        def _():
            for side, (q_out, k_out, v_out) in ((which, (qs, ks, vs)), (1 - which, (qo, ko, vo))):
                cols = slice(side * HD, side * HD + HD)
                q_out[...] = rot(q[:, cols], cq[...], sq[...]).T.astype(bf16)
                k_out[...] = rot(k[:, cols], ck[...], sk[...]).astype(bf16)
                v_out[...] = v[:, cols]


def fill_keys(at, k_own, k_par, kaug):
    rows = k_own.shape[0]
    lane = lax.broadcasted_iota(jnp.int32, (rows, HD), 1)
    row = lax.broadcasted_iota(jnp.int32, (rows, HD), 0)
    ones = jnp.where((lane >= 3) & (lane < 6), 1.0, 0.0)
    for part, ref in enumerate((k_own, k_par)):
        bias = jnp.where(row + at[1 + part] < at[3], 0.0, DEAD)
        kaug[part * rows : part * rows + rows, :HD] = ref[...]
        kaug[part * rows : part * rows + rows, HD:] = jnp.where(lane == 6, bias, ones).astype(bf16)


def forward_kernel(at, *refs, blocks):
    q_refs = refs[:blocks]
    k_own, k_par, v_own, v_par = refs[blocks : blocks + 4]
    out_refs = refs[blocks + 4 : 2 * blocks + 4]
    kaug, v_t, q_all, out_all, scores = refs[2 * blocks + 4 :]
    rows = k_own.shape[0]
    keys = 2 * rows
    wide = q_refs[0].shape[1]
    fill_keys(at, k_own, k_par, kaug)
    v_t[:, :rows] = v_own[...].astype(f32).T.astype(bf16)
    v_t[:, rows:] = v_par[...].astype(f32).T.astype(bf16)
    sub = lax.broadcasted_iota(jnp.int32, (HD, wide), 0)
    tail = jnp.where(sub == 6, 1.0, 0.0).astype(bf16)
    for i in range(blocks):
        q_all[i, :HD, :] = q_refs[i][...]
        q_all[i, HD:, :] = tail

    def block(i, carry):
        query = q_all[i]
        top = jnp.full((1, wide), -jnp.inf, f32)
        for j in range(keys // CHUNK):
            part = slice(j * CHUNK, j * CHUNK + CHUNK)
            s = dot(kaug[part, :], query, NN)
            scores[part, :] = s
            top = jnp.maximum(top, jnp.max(s, axis=0, keepdims=True))
        total = jnp.zeros((1, wide), f32)
        acc = jnp.zeros((HD, wide), f32)
        for j in range(keys // CHUNK):
            part = slice(j * CHUNK, j * CHUNK + CHUNK)
            p = jnp.exp2((scores[part, :] - top) * EXP2_SCALE)
            total = total + jnp.sum(p, axis=0, keepdims=True)
            acc = acc + dot(v_t[:, part], p.astype(bf16), NN)
        out_all[i, :HD, :] = (acc / total).astype(bf16)
        log_sum = top + jnp.log(total) * (1.0 / SCALE)
        high, middle, low = split3(log_sum)
        which = lax.broadcasted_iota(jnp.int32, (EXTRA, wide), 0)
        pieces = jnp.where(which == 0, high, jnp.where(which == 1, middle, jnp.where(which == 2, low, 0.0)))
        out_all[i, HD:, :] = pieces.astype(bf16)
        return carry

    lax.fori_loop(0, blocks, block, 0)
    for i in range(blocks):
        out_refs[i][...] = out_all[i]


def forward(at, q_blocks, k_own, k_par, v_own, v_par):
    blocks = len(q_blocks)
    wide = q_blocks[0].shape[1]
    keys = 2 * k_own.shape[0]
    return call(
        functools.partial(forward_kernel, blocks=blocks),
        [SMEM] + [VMEM] * (blocks + 4),
        [((HD + EXTRA, wide), bf16)] * blocks,
        [
            pltpu.VMEM((keys, 2 * HD), bf16),
            pltpu.VMEM((HD, keys), bf16),
            pltpu.VMEM((blocks, 2 * HD, wide), bf16),
            pltpu.VMEM((blocks, HD + EXTRA, wide), bf16),
            pltpu.VMEM((keys, wide), f32),
        ],
    )(at, *q_blocks, k_own, k_par, v_own, v_par)


def one_hot(place):
    rows = place.shape[1]
    row = lax.broadcasted_iota(jnp.int32, (rows, rows), 0)
    return jnp.where(row == place[...], 1.0, 0.0).astype(bf16)


def combine_kernel(at, place, *refs):
    partial, (out_t, logs, c0, c1, c2, c3) = refs[:8], refs[8:]
    wide = partial[0].shape[1]
    for side in range(2):
        sums = []
        for ref in partial[4 * side : 4 * side + 4]:
            tail = ref[HD:, :].astype(f32)
            sums.append(tail[0:1] + tail[1:2] + tail[2:3])
        top = functools.reduce(jnp.maximum, sums)
        weight = [jnp.exp2((s - top) * EXP2_SCALE) for s in sums]
        total = sum(weight)
        acc = jnp.zeros((HD, wide), f32)
        for w, ref in zip(weight, partial[4 * side : 4 * side + 4]):
            acc = acc + (w / total) * ref[:HD, :].astype(f32)
        logs[side, :, :] = jnp.broadcast_to(top + jnp.log(total) * (1.0 / SCALE), (8, wide))
        head = at[0] if side == 0 else 1 - at[0]
        out_t[pl.ds(pl.multiple_of(head * HD, HD), HD), :] = acc.astype(bf16)
    grouped = dot(one_hot(place), out_t[...], NT).astype(bf16)
    quarter = wide // 4
    for i, ref in enumerate((c0, c1, c2, c3)):
        ref[...] = grouped[i * quarter : i * quarter + quarter]


def project_kernel(o0, o1, o2, o3, w0, w1, w2, w3, x0, x1, x2, x3):
    total = None
    for o, w in ((o0, w0), (o1, w1), (o2, w2), (o3, w3)):
        term = dot(o[...], w[...], NN)
        total = term if total is None else total + term
    rows = x0.shape[0]
    for i, ref in enumerate((x0, x1, x2, x3)):
        ref[...] = total[i * rows : i * rows + rows].astype(ref.dtype)


def unproject_kernel(g0, g1, g2, g3, w0, w1, w2, w3, d0, d1, d2, d3, g):
    rows = g0.shape[0]
    for i, ref in enumerate((g0, g1, g2, g3)):
        g[i * rows : i * rows + rows, :] = ref[...]
    for w, d in ((w0, d0), (w1, d1), (w2, d2), (w3, d3)):
        d[...] = dot(g[...], w[...], NT).astype(bf16)


def center(x):
    mean = jnp.mean(x, axis=1, keepdims=True)
    shifted = x - mean
    rate = lax.rsqrt(jnp.mean(shifted * shifted, axis=1, keepdims=True) + EPSILON)
    return shifted * rate, rate


def center_grad(grad, normed, rate):
    return rate * (
        grad
        - jnp.mean(grad, axis=1, keepdims=True)
        - normed * jnp.mean(grad * normed, axis=1, keepdims=True)
    )


def reward_kernel(x0, x1, x2, x3, live, head, up_hbm, down_hbm, grad_out, reward_out, up, down, sems):
    up_copy = pltpu.make_async_copy(up_hbm, up, sems.at[0])
    down_copy = pltpu.make_async_copy(down_hbm, down, sems.at[1])
    up_copy.start()
    down_copy.start()
    x = x0[...].astype(f32) + x1[...].astype(f32) + x2[...].astype(f32) + x3[...].astype(f32)
    normed, rate = center(x)
    up_copy.wait()
    before = dot(normed.astype(bf16), up[...], NN)
    c0 = math.sqrt(2.0 / math.pi)
    c1 = 0.044715
    square = before * before
    tanh = jnp.tanh(c0 * before * (1.0 + c1 * square))
    half = 0.5 * (1.0 + tanh)
    expanded = (before * half).astype(bf16)
    slope = half + 0.5 * before * (1.0 - tanh * tanh) * (c0 * (1.0 + 3.0 * c1 * square))
    down_copy.wait()
    hidden = dot(expanded, down[...], NN)
    alive = live[...]
    count = jnp.sum(alive[:, :1], axis=0, keepdims=True)
    pooled = jnp.sum(hidden * alive[:, :1], axis=0, keepdims=True) / count
    pooled_normed, pooled_rate = center(pooled)
    reward = count * jnp.sum(pooled_normed * head[...], axis=1, keepdims=True)
    reward_out[...] = jnp.broadcast_to(reward, reward_out.shape)
    pooled_grad = center_grad(count * head[...], pooled_normed, pooled_rate) / count
    high, middle, low = split3(pooled_grad)
    which = lax.broadcasted_iota(jnp.int32, (EXTRA, pooled_grad.shape[1]), 0)
    pieces = jnp.where(which == 0, high, jnp.where(which == 1, middle, jnp.where(which == 2, low, 0.0)))
    spread = jnp.sum(dot(pieces.astype(bf16), down[...], NT), axis=0, keepdims=True)
    before_grad = alive[:, :1] * spread * slope
    normed_grad = dot(before_grad.astype(bf16), up[...], NT)
    grad_out[...] = center_grad(normed_grad, normed, rate).astype(bf16)


def ungroup_kernel(at, place, d0, d1, d2, d3, out_t, logs, ps, po, grad):
    quarter = d0.shape[0]
    for i, ref in enumerate((d0, d1, d2, d3)):
        grad[i * quarter : i * quarter + quarter, :] = ref[...]
    wide = place.shape[1]
    grad_t = dot(grad[...], one_hot(place), TN)
    product = grad_t * out_t[...].astype(f32)
    which = lax.broadcasted_iota(jnp.int32, (EXTRA, wide), 0)
    for head in range(2):
        delta = jnp.sum(product[head * HD : head * HD + HD], axis=0, keepdims=True)
        for side, ref in enumerate((ps, po)):

            @pl.when(head == (at[0] if side == 0 else 1 - at[0]))
            def _():
                ref[:HD, :] = grad_t[head * HD : head * HD + HD].astype(bf16)
                rows = split3(delta) + split3(-logs[side, 0:1, :])
                tail = jnp.where(which == 6, 1.0, 0.0)
                for i, piece in enumerate(rows):
                    tail = jnp.where(which == i, piece, tail)
                ref[HD:, :] = tail.astype(bf16)


def backward_kernel(at, *refs, blocks):
    q_refs = refs[:blocks]
    g_refs = refs[blocks : 2 * blocks]
    k_own, k_par, v_own, v_par = refs[2 * blocks : 2 * blocks + 4]
    dq_refs = refs[2 * blocks + 4 : 3 * blocks + 4]
    dk_own, dv_own, dk_par, dv_par = refs[3 * blocks + 4 : 3 * blocks + 8]
    kaug, vaug, k_t, q_all, g_all, dq_all, dk, dv = refs[3 * blocks + 8 :]
    rows = k_own.shape[0]
    keys = 2 * rows
    wide = q_refs[0].shape[1]
    fill_keys(at, k_own, k_par, kaug)
    lane = lax.broadcasted_iota(jnp.int32, (rows, HD), 1)
    minus = jnp.where(lane < 3, -1.0, 0.0).astype(bf16)
    for part, (k_ref, v_ref) in enumerate(((k_own, v_own), (k_par, v_par))):
        where = slice(part * rows, part * rows + rows)
        vaug[where, :HD] = v_ref[...]
        vaug[where, HD:] = minus
        k_t[:, where] = k_ref[...].astype(f32).T.astype(bf16)
    dk[...] = jnp.zeros_like(dk)
    dv[...] = jnp.zeros_like(dv)
    blank = jnp.zeros((HD - EXTRA, wide), bf16)
    for i in range(blocks):
        q_all[i, :HD, :] = q_refs[i][...]
        q_all[i, HD : HD + EXTRA, :] = g_refs[i][HD:, :]
        q_all[i, HD + EXTRA :, :] = blank
        g_all[i, : HD + EXTRA, :] = g_refs[i][...]
        g_all[i, HD + EXTRA :, :] = blank

    def block(i, carry):
        query = q_all[i]
        grad = g_all[i]
        acc = jnp.zeros((HD, wide), f32)
        for j in range(keys // CHUNK):
            part = slice(j * CHUNK, j * CHUNK + CHUNK)
            p = jnp.exp2(dot(kaug[part, :], query, NN) * EXP2_SCALE)
            ds = (p * dot(vaug[part, :], grad, NN)).astype(bf16)
            dv[part, :] += dot(p.astype(bf16), grad[:HD], NT)
            dk[part, :] += dot(ds, query[:HD], NT)
            acc = acc + dot(k_t[:, part], ds, NN)
        dq_all[i] = (acc * SCALE).astype(bf16)
        return carry

    lax.fori_loop(0, blocks, block, 0)
    for i in range(blocks):
        dq_refs[i][...] = dq_all[i]
    dk_own[...] = dk[:rows, :] * SCALE
    dk_par[...] = (dk[rows:, :] * SCALE).astype(bf16)
    dv_own[...] = dv[:rows, :]
    dv_par[...] = dv[rows:, :].astype(bf16)


def backward(at, q_blocks, g_blocks, k_own, k_par, v_own, v_par):
    blocks = len(q_blocks)
    wide = q_blocks[0].shape[1]
    rows = k_own.shape[0]
    keys = 2 * rows
    out = call(
        functools.partial(backward_kernel, blocks=blocks),
        [SMEM] + [VMEM] * (2 * blocks + 4),
        [((HD, wide), bf16)] * blocks + [((rows, HD), f32)] * 2 + [((rows, HD), bf16)] * 2,
        [
            pltpu.VMEM((keys, 2 * HD), bf16),
            pltpu.VMEM((keys, 2 * HD), bf16),
            pltpu.VMEM((HD, keys), bf16),
            pltpu.VMEM((blocks, 2 * HD, wide), bf16),
            pltpu.VMEM((blocks, 2 * HD, wide), bf16),
            pltpu.VMEM((blocks, HD, wide), bf16),
            pltpu.VMEM((keys, HD), f32),
            pltpu.VMEM((keys, HD), f32),
        ],
    )(at, *q_blocks, *g_blocks, k_own, k_par, v_own, v_par)
    return out[:blocks], out[blocks:]


def unrotate(x, c, s):
    return x * c - pltpu.roll(x, HD // 2, 1) * s


def query_grad_kernel(at, c, s, *refs):
    parts, (out,) = refs[:8], refs[8:]
    for which in range(2):

        @pl.when(at[0] == which)
        def _():
            for side in range(2):
                total = sum(ref[...].astype(f32) for ref in parts[4 * side : 4 * side + 4])
                head = which if side == 0 else 1 - which
                out[:, head * HD : head * HD + HD] = unrotate(total.T, c[...], s[...])


def key_grad_kernel(at, c, s, dk_own, dk_par, dv_own, dv_par, dk_out, dv_out):
    for which in range(2):

        @pl.when(at[0] == which)
        def _():
            for head, dk, dv in ((which, dk_own, dv_own), (1 - which, dk_par, dv_par)):
                cols = slice(head * HD, head * HD + HD)
                dk_out[:, cols] = unrotate(dk[...].astype(f32), c[...], s[...])
                dv_out[:, cols] = dv[...].astype(f32)


def ctx_shift(dx, dz):
    return [
        (x * 2 + z, ((x + dx) % 4) * 2 + (z + dz) % 2) for x in range(4) for z in range(2)
    ]


def frame_xor(mask):
    return [(i, i ^ mask) for i in range(16)]


QUAD_MASKS = (0, 1, 8, 9)
Y_MASKS = (0, 2, 4, 6)
SHIFTS = tuple((dx, dz) for dz in range(2) for dx in range(4))


def send_frame(array, mask):
    return array if mask == 0 else lax.ppermute(array, "frame", frame_xor(mask))


def send_ctx(array, dx, dz):
    return array if dx % 4 == 0 and dz % 2 == 0 else lax.ppermute(array, "ctx", ctx_shift(dx, dz))


def tables(position):
    half_width = HD // 2
    frequency = jnp.exp(-math.log(10000.0) * jnp.arange(half_width, dtype=f32) / half_width)
    frequency = jnp.concatenate([frequency, frequency])
    sign = jnp.where(jnp.arange(HD) < half_width, -1.0, 1.0).astype(f32)
    angle = position.astype(f32)[:, None] * frequency[None, :]
    return jnp.cos(angle), jnp.sin(angle) * sign[None, :]


def shards(
    queries,
    keys,
    values,
    query_frames,
    frame_counts,
    clip_of_frame,
    in_proj,
    mlp_up,
    mlp_down,
    reward_head,
):
    ctx_index = lax.axis_index("ctx")
    frame_index = lax.axis_index("frame")
    query_rows = queries.shape[0]
    key_rows = keys.shape[0]
    frame_slots = query_frames.shape[0]
    key_frames = frame_counts.shape[0]
    in_frame = jnp.arange(FTOK, dtype=jnp.int32)
    query_position = (query_frames[:, None] * FTOK + in_frame[None, :]).reshape(-1)
    key_position = ctx_index * key_rows + jnp.arange(key_rows, dtype=jnp.int32)
    cq, sq = tables(query_position)
    ck, sk = tables(key_position)
    at = jnp.stack(
        [
            ctx_index % 2,
            ctx_index * key_rows,
            (ctx_index ^ 1) * key_rows,
            jnp.sum(frame_counts),
        ]
    ).astype(jnp.int32)

    half = (HD, query_rows)
    part = (key_rows, HD)
    qs, qo, k_own, k_send, v_own, v_send = call(
        rotate_kernel,
        [SMEM] + [VMEM] * 7,
        [(half, bf16)] * 2 + [(part, bf16)] * 4,
    )(at, queries, keys, values, cq, sq, ck, sk)
    k_par = send_ctx(k_send, 0, 1)
    q_blocks = [send_ctx(qo if dz else qs, dx, dz) for dx, dz in SHIFTS]
    v_par = send_ctx(v_send, 0, 1)
    near = send_frame(in_proj, 8)
    weights = (in_proj, send_frame(in_proj, 1), near, send_frame(near, 1))

    slot_index = jnp.arange(frame_slots, dtype=jnp.int32)
    same_clip = clip_of_frame[:, None] == clip_of_frame[None, :]
    earlier = slot_index[None, :] < slot_index[:, None]
    rank = jnp.sum(jnp.logical_and(same_clip, earlier), axis=1).astype(jnp.int32)
    away = clip_of_frame ^ frame_index
    quad = (away >> 3) * 2 + (away & 1)
    slot_place = (quad * 4 + ((away >> 1) & 3)) * CLIP + rank
    place = (slot_place[:, None] * FTOK + in_frame[None, :]).reshape(1, query_rows)
    frame_match = query_frames[:, None] == jnp.arange(key_frames, dtype=jnp.int32)[None, :]
    slot_counts = jnp.sum(jnp.where(frame_match, frame_counts[None, :], 0), axis=1)
    mine = slot_place[None, :] == jnp.arange(CLIP, dtype=jnp.int32)[:, None]
    my_counts = jnp.sum(jnp.where(mine, slot_counts[None, :], 0), axis=1)
    clip_live = (in_frame[None, :] < my_counts[:, None]).reshape(-1).astype(f32)
    clip_live = jnp.broadcast_to(clip_live[:, None], (CLIP * FTOK, HD))

    partial = forward(at, q_blocks, k_own, k_par, v_own, v_par)
    partial = [send_ctx(block, -dx, -dz) for block, (dx, dz) in zip(partial, SHIFTS)]
    width = queries.shape[1]
    quarter = query_rows // 4
    out_t, logs, *chunks = call(
        combine_kernel,
        [SMEM] + [VMEM] * 9,
        [((width, query_rows), bf16), ((2, 8, query_rows), f32)] + [((quarter, width), bf16)] * 4,
    )(at, place, *partial)
    chunks = [send_frame(chunk, mask) for chunk, mask in zip(chunks, QUAD_MASKS)]
    vision = in_proj.shape[1]
    clip_rows = CLIP * FTOK
    inputs = call(
        project_kernel,
        [VMEM] * 8,
        [((clip_rows, vision), f32)] + [((clip_rows, vision), bf16)] * 3,
    )(*chunks, *weights)
    inputs = [send_frame(x, mask) for x, mask in zip(inputs, Y_MASKS)]
    any_spec = pl.BlockSpec(memory_space=pl.ANY)
    input_grad, reward = call(
        reward_kernel,
        [VMEM] * 6 + [any_spec] * 2,
        [((clip_rows, vision), bf16), ((8, HD), f32)],
        [
            pltpu.VMEM(mlp_up.shape, bf16),
            pltpu.VMEM(mlp_down.shape, bf16),
            pltpu.SemaphoreType.DMA((2,)),
        ],
    )(*inputs, clip_live, reward_head.reshape(1, -1), mlp_up, mlp_down)
    grads = [send_frame(input_grad, mask) for mask in Y_MASKS]
    grads = call(
        unproject_kernel,
        [VMEM] * 8,
        [((quarter, width), bf16)] * 4,
        [pltpu.VMEM((quarter, vision), bf16)],
    )(*grads, *weights)
    grads = [send_frame(grad, mask) for grad, mask in zip(grads, QUAD_MASKS)]
    packed = (HD + EXTRA, query_rows)
    gs, go = call(
        ungroup_kernel,
        [SMEM] + [VMEM] * 7,
        [(packed, bf16)] * 2,
        [pltpu.VMEM((query_rows, width), bf16)],
    )(at, place, *grads, out_t, logs)
    g_blocks = [send_ctx(go if dz else gs, dx, dz) for dx, dz in SHIFTS]
    dq_blocks, (dk_own, dv_own, dk_send, dv_send) = backward(
        at, q_blocks, g_blocks, k_own, k_par, v_own, v_par
    )
    dq_blocks = [send_ctx(block, -dx, -dz) for block, (dx, dz) in zip(dq_blocks, SHIFTS)]
    dk_par = send_ctx(dk_send, 0, 1)
    dv_par = send_ctx(dv_send, 0, 1)
    key_grad, value_grad = call(
        key_grad_kernel,
        [SMEM] + [VMEM] * 6,
        [((key_rows, width), f32)] * 2,
    )(at, ck, sk, dk_own, dk_par, dv_own, dv_par)
    (query_grad,) = call(
        query_grad_kernel,
        [SMEM] + [VMEM] * 10,
        [((query_rows, width), f32)],
    )(at, cq, sq, *dq_blocks)
    return query_grad, key_grad, value_grad, reward[0, :1]


def solution(mesh):
    return jax.shard_map(
        shards,
        mesh=mesh,
        in_specs=(
            P("ctx", "frame"),
            P("ctx", "frame"),
            P("ctx", "frame"),
            P("ctx"),
            P(),
            P("ctx"),
            P("frame", None),
            P(),
            P(),
            P(),
        ),
        out_specs=(P("ctx", "frame"), P("ctx", "frame"), P("ctx", "frame"), P(("ctx", "frame"))),
        check_vma=False,
    )
```

```python
import functools
import math

import jax
import jax.numpy as jnp
from jax import lax
from jax.experimental import pallas as pl
from jax.experimental.pallas import tpu as pltpu
from jax.sharding import PartitionSpec as P

HD = 128
FTOK = 16
CLIP = 2
EPSILON = 1e-05
SCALE = 1.0 / math.sqrt(HD)
EXP2_SCALE = SCALE * math.log2(math.e)
DEAD = -1e30
EXTRA = 16
CHUNK = 512


f32 = jnp.float32
bf16 = jnp.bfloat16

NN = (((1,), (0,)), ((), ()))
NT = (((1,), (1,)), ((), ()))
TN = (((0,), (0,)), ((), ()))

VMEM = pl.BlockSpec(memory_space=pltpu.VMEM)
SMEM = pl.BlockSpec(memory_space=pltpu.SMEM)


def dot(left, right, dims):
    return lax.dot_general(left, right, dims, preferred_element_type=f32)


def call(kernel, in_specs, outs, scratch=(), work=0):
    return pl.pallas_call(
        kernel,
        cost_estimate=pl.CostEstimate(flops=work, transcendentals=0, bytes_accessed=1 << 20),
        out_shape=[jax.ShapeDtypeStruct(shape, dtype) for shape, dtype in outs],
        in_specs=in_specs,
        out_specs=[VMEM] * len(outs),
        scratch_shapes=list(scratch),
        compiler_params=pltpu.CompilerParams(vmem_limit_bytes=56 * 1024 * 1024),
    )


def split3(x):
    high = x.astype(bf16).astype(f32)
    rest = x - high
    middle = rest.astype(bf16).astype(f32)
    low = (rest - middle).astype(bf16).astype(f32)
    return high, middle, low


def spread_angles(cf, sf, ct, st):
    c = cf[:, None, :] * ct[...][None] - sf[:, None, :] * st[...][None]
    s = sf[:, None, :] * ct[...][None] + cf[:, None, :] * st[...][None]
    rows = cf.shape[0] * FTOK
    lane = lax.broadcasted_iota(jnp.int32, (rows, HD), 1)
    return c.reshape(rows, HD), jnp.where(lane < HD // 2, -1.0, 1.0) * s.reshape(rows, HD)


def query_angles(cf, sf, ct, st, slots):
    return spread_angles(cf[:slots, :], sf[:slots, :], ct, st)


def key_angles(cf, sf, ct, st, slots):
    return spread_angles(cf[-slots:, :], sf[-slots:, :], ct, st)


def rotate_query_kernel(z, x, cf, sf, ct, st, own, other):
    c, s = query_angles(cf, sf, ct, st, x.shape[0] // FTOK)
    for which in range(2):

        @pl.when(z[0] == which)
        def _():
            for side, out in ((which, own), (1 - which, other)):
                head = x[:, side * HD : side * HD + HD].astype(f32)
                turned = head * c + pltpu.roll(head, HD // 2, 1) * s
                out[...] = turned.T.astype(bf16)


def rotate_key_kernel(z, x, v, cf, sf, ct, st, own, other):
    c, s = key_angles(cf, sf, ct, st, x.shape[0] // FTOK)
    for which in range(2):

        @pl.when(z[0] == which)
        def _():
            for side, out in ((which, own), (1 - which, other)):
                cols = slice(side * HD, side * HD + HD)
                head = x[:, cols].astype(f32)
                turned = head * c + pltpu.roll(head, HD // 2, 1) * s
                out[:, :HD] = turned.astype(bf16)
                out[:, HD:] = v[:, cols]


def fill_keys(at, starts, kv_refs, kaug):
    rows = kv_refs[0].shape[0]
    lane = lax.broadcasted_iota(jnp.int32, (rows, HD), 1)
    row = lax.broadcasted_iota(jnp.int32, (rows, HD), 0)
    ones = jnp.where((lane >= 3) & (lane < 6), 1.0, 0.0)
    for part, ref in enumerate(kv_refs):
        bias = jnp.where(row + at[starts[part]] < at[0], 0.0, DEAD)
        kaug[part * rows : part * rows + rows, :HD] = ref[:, :HD]
        kaug[part * rows : part * rows + rows, HD:] = jnp.where(lane == 6, bias, ones).astype(bf16)


def forward_kernel(at, *refs, blocks, starts, first):
    refs = list(refs)

    def take(count):
        taken = refs[:count]
        del refs[:count]
        return taken

    pieces = len(starts)
    q_refs = take(blocks)
    kv_refs = take(pieces)
    if not first:
        acc_in, stat_in = take(2)
    if first:
        acc_out, stat_out = take(2)
    else:
        out_refs = take(blocks)
    kaug, v_t, q_all, *scores = take(5)
    rows = kv_refs[0].shape[0]
    keys = pieces * rows
    wide = q_refs[0].shape[1]
    fill_keys(at, starts, kv_refs, kaug)
    for part, ref in enumerate(kv_refs):
        v_t[:, part * rows : part * rows + rows] = ref[:, HD:].astype(f32).T.astype(bf16)
    sub = lax.broadcasted_iota(jnp.int32, (HD, wide), 0)
    tail = jnp.where(sub == 6, 1.0, 0.0).astype(bf16)
    for i in range(blocks):
        q_all[i, :HD, :] = q_refs[i][...]
        q_all[i, HD:, :] = tail
    spans = [slice(j * CHUNK, j * CHUNK + CHUNK) for j in range(keys // CHUNK)]

    def score(i, slot, span, top):
        s = dot(kaug[span, :], q_all[i], NN)
        scores[slot][span, :] = s
        return jnp.maximum(top, jnp.max(s, axis=0, keepdims=True))

    def start(i):
        return jnp.full((1, wide), -jnp.inf, f32) if first else stat_in[i, 0:1, :]

    def block(i, top, follow):
        slot = i % 2
        if first:
            total = jnp.zeros((1, wide), f32)
            acc = jnp.zeros((HD, wide), f32)
        else:
            shrink = jnp.exp2((stat_in[i, 0:1, :] - top) * EXP2_SCALE)
            total = stat_in[i, 1:2, :] * shrink
            acc = acc_in[i] * shrink
        following = start(i + 1) if follow else top
        for span in spans:
            if follow:
                following = score(i + 1, 1 - slot, span, following)
            p = jnp.exp2((scores[slot][span, :] - top) * EXP2_SCALE)
            total = total + jnp.sum(p, axis=0, keepdims=True)
            acc = acc + dot(v_t[:, span], p.astype(bf16), NN)
        if first:
            acc_out[i] = acc
            which = lax.broadcasted_iota(jnp.int32, (8, wide), 0)
            stat_out[i] = jnp.where(which == 0, top, total)
        else:
            out_refs[i][:HD, :] = (acc / total).astype(bf16)
            high, middle, low = split3(top + jnp.log(total) * (1.0 / SCALE))
            which = lax.broadcasted_iota(jnp.int32, (EXTRA, wide), 0)
            rest = jnp.where(which == 1, middle, jnp.where(which == 2, low, 0.0))
            out_refs[i][HD:, :] = jnp.where(which == 0, high, rest).astype(bf16)
        return following

    top = start(0)
    for span in spans:
        top = score(0, 0, span, top)
    for i in range(blocks):
        top = block(i, top, i + 1 < blocks)


def forward(at, q_blocks, kv_pieces, starts, before=None):
    blocks = len(q_blocks)
    wide = q_blocks[0].shape[1]
    keys = len(kv_pieces) * kv_pieces[0].shape[0]
    first = before is None
    if first:
        outs = [((blocks, HD, wide), f32), ((blocks, 8, wide), f32)]
    else:
        outs = [((HD + EXTRA, wide), bf16)] * blocks
    args = [*q_blocks, *kv_pieces] + ([] if first else list(before))
    return call(
        functools.partial(forward_kernel, blocks=blocks, starts=starts, first=first),
        [SMEM] + [VMEM] * len(args),
        outs,
        [
            pltpu.VMEM((keys, 2 * HD), bf16),
            pltpu.VMEM((HD, keys), bf16),
            pltpu.VMEM((blocks, 2 * HD, wide), bf16),
            pltpu.VMEM((keys, wide), f32),
            pltpu.VMEM((keys, wide), f32),
        ],
        work=10**10,
    )(at, *args)


def one_hot(place):
    rows = place.shape[1]
    row = lax.broadcasted_iota(jnp.int32, (rows, rows), 0)
    return jnp.where(row == place[...], 1.0, 0.0).astype(bf16)


def combine_kernel(z, place, *refs):
    partial, (out_t, logs, c0, c1, c2, c3) = refs[:4], refs[4:]
    wide = partial[0].shape[1]
    for side in range(2):
        sums = []
        for ref in partial[2 * side : 2 * side + 2]:
            tail = ref[HD:, :].astype(f32)
            sums.append(tail[0:1] + tail[1:2] + tail[2:3])
        top = functools.reduce(jnp.maximum, sums)
        weight = [jnp.exp2((s - top) * EXP2_SCALE) for s in sums]
        total = sum(weight)
        acc = jnp.zeros((HD, wide), f32)
        for w, ref in zip(weight, partial[2 * side : 2 * side + 2]):
            acc = acc + (w / total) * ref[:HD, :].astype(f32)
        logs[side, :, :] = jnp.broadcast_to(top + jnp.log(total) * (1.0 / SCALE), (8, wide))
        head = z[0] if side == 0 else 1 - z[0]
        out_t[pl.ds(pl.multiple_of(head * HD, HD), HD), :] = acc.astype(bf16)
    grouped = dot(one_hot(place), out_t[...], NT).astype(bf16)
    quarter = wide // 4
    for i, ref in enumerate((c0, c1, c2, c3)):
        ref[...] = grouped[i * quarter : i * quarter + quarter]


def project_kernel(o0, o1, o2, o3, w0, w1, w2, w3, x0, x1, x2, x3):
    total = None
    for o, w in ((o0, w0), (o1, w1), (o2, w2), (o3, w3)):
        term = dot(o[...], w[...], NN)
        total = term if total is None else total + term
    rows = x0.shape[0]
    for i, ref in enumerate((x0, x1, x2, x3)):
        ref[...] = total[i * rows : i * rows + rows].astype(ref.dtype)


def unproject_kernel(g0, g1, g2, g3, w0, w1, w2, w3, d0, d1, d2, d3, g):
    rows = g0.shape[0]
    for i, ref in enumerate((g0, g1, g2, g3)):
        g[i * rows : i * rows + rows, :] = ref[...]
    for w, d in ((w0, d0), (w1, d1), (w2, d2), (w3, d3)):
        d[...] = dot(g[...], w[...], NT).astype(bf16)


def center(x):
    mean = jnp.mean(x, axis=1, keepdims=True)
    shifted = x - mean
    rate = lax.rsqrt(jnp.mean(shifted * shifted, axis=1, keepdims=True) + EPSILON)
    return shifted * rate, rate


def center_grad(grad, normed, rate):
    return rate * (
        grad
        - jnp.mean(grad, axis=1, keepdims=True)
        - normed * jnp.mean(grad * normed, axis=1, keepdims=True)
    )


def reward_kernel(x0, x1, x2, x3, live, head, up_hbm, down_hbm, grad_out, reward_out, up, down, sems):
    up_copy = pltpu.make_async_copy(up_hbm, up, sems.at[0])
    down_copy = pltpu.make_async_copy(down_hbm, down, sems.at[1])
    up_copy.start()
    down_copy.start()
    x = x0[...].astype(f32) + x1[...].astype(f32) + x2[...].astype(f32) + x3[...].astype(f32)
    normed, rate = center(x)
    up_copy.wait()
    before = dot(normed.astype(bf16), up[...], NN)
    c0 = math.sqrt(2.0 / math.pi)
    c1 = 0.044715
    square = before * before
    tanh = jnp.tanh(c0 * before * (1.0 + c1 * square))
    half = 0.5 * (1.0 + tanh)
    expanded = (before * half).astype(bf16)
    slope = half + 0.5 * before * (1.0 - tanh * tanh) * (c0 * (1.0 + 3.0 * c1 * square))
    down_copy.wait()
    hidden = dot(expanded, down[...], NN)
    alive = live[...]
    count = jnp.sum(alive[:, :1], axis=0, keepdims=True)
    pooled = jnp.sum(hidden * alive[:, :1], axis=0, keepdims=True) / count
    pooled_normed, pooled_rate = center(pooled)
    reward = count * jnp.sum(pooled_normed * head[...], axis=1, keepdims=True)
    reward_out[...] = jnp.broadcast_to(reward, reward_out.shape)
    pooled_grad = center_grad(count * head[...], pooled_normed, pooled_rate) / count
    high, middle, low = split3(pooled_grad)
    which = lax.broadcasted_iota(jnp.int32, (EXTRA, pooled_grad.shape[1]), 0)
    pieces = jnp.where(which == 0, high, jnp.where(which == 1, middle, jnp.where(which == 2, low, 0.0)))
    spread = jnp.sum(dot(pieces.astype(bf16), down[...], NT), axis=0, keepdims=True)
    before_grad = alive[:, :1] * spread * slope
    normed_grad = dot(before_grad.astype(bf16), up[...], NT)
    grad_out[...] = center_grad(normed_grad, normed, rate).astype(bf16)


def ungroup_kernel(z, place, d0, d1, d2, d3, out_t, logs, ps, po, grad):
    quarter = d0.shape[0]
    for i, ref in enumerate((d0, d1, d2, d3)):
        grad[i * quarter : i * quarter + quarter, :] = ref[...]
    wide = place.shape[1]
    grad_t = dot(grad[...], one_hot(place), TN)
    product = grad_t * out_t[...].astype(f32)
    which = lax.broadcasted_iota(jnp.int32, (EXTRA, wide), 0)
    for head in range(2):
        delta = jnp.sum(product[head * HD : head * HD + HD], axis=0, keepdims=True)
        for side, ref in enumerate((ps, po)):

            @pl.when(head == (z[0] if side == 0 else 1 - z[0]))
            def _():
                ref[:HD, :] = grad_t[head * HD : head * HD + HD].astype(bf16)
                rows = split3(delta) + split3(-logs[side, 0:1, :])
                tail = jnp.where(which == 6, 1.0, 0.0)
                for i, piece in enumerate(rows):
                    tail = jnp.where(which == i, piece, tail)
                ref[HD:, :] = tail.astype(bf16)


def backward_kernel(at, *refs, blocks, starts, first, last):
    refs = list(refs)

    def take(count):
        taken = refs[:count]
        del refs[:count]
        return taken

    pieces = len(starts)
    q_refs = take(blocks)
    g_refs = take(blocks)
    kv_refs = take(pieces)
    if not first:
        (dq_in,) = take(1)
    dq_refs = take(blocks) if last else take(1)
    out_refs = take(pieces + 1) if last else take(pieces)
    kaug, vaug, k_t, q_all, g_all, dk, dv = take(7)
    if last:
        (dq_all,) = take(1)
    rows = kv_refs[0].shape[0]
    keys = pieces * rows
    wide = q_refs[0].shape[1]
    fill_keys(at, starts, kv_refs, kaug)
    lane = lax.broadcasted_iota(jnp.int32, (rows, HD), 1)
    minus = jnp.where(lane < 3, -1.0, 0.0).astype(bf16)
    for part, ref in enumerate(kv_refs):
        where = slice(part * rows, part * rows + rows)
        vaug[where, :HD] = ref[:, HD:]
        vaug[where, HD:] = minus
        k_t[:, where] = ref[:, :HD].astype(f32).T.astype(bf16)
    dk[...] = jnp.zeros_like(dk)
    dv[...] = jnp.zeros_like(dv)
    blank = jnp.zeros((HD - EXTRA, wide), bf16)
    for i in range(blocks):
        q_all[i, :HD, :] = q_refs[i][...]
        q_all[i, HD : HD + EXTRA, :] = g_refs[i][HD:, :]
        q_all[i, HD + EXTRA :, :] = blank
        g_all[i, : HD + EXTRA, :] = g_refs[i][...]
        g_all[i, HD + EXTRA :, :] = blank

    def block(i, carry):
        query = q_all[i]
        grad = g_all[i]
        acc = jnp.zeros((HD, wide), f32) if first else dq_in[i]
        for j in range(keys // CHUNK):
            part = slice(j * CHUNK, j * CHUNK + CHUNK)
            p = jnp.exp2(dot(kaug[part, :], query, NN) * EXP2_SCALE)
            ds = (p * dot(vaug[part, :], grad, NN)).astype(bf16)
            dv[part, :] += dot(p.astype(bf16), grad[:HD], NT)
            dk[part, :] += dot(ds, query[:HD], NT)
            acc = acc + dot(k_t[:, part], ds, NN)
        if last:
            dq_all[i] = (acc * SCALE).astype(bf16)
        else:
            dq_refs[0][i] = acc
        return carry

    lax.fori_loop(0, blocks, block, 0)
    if last:
        for i in range(blocks):
            dq_refs[i][...] = dq_all[i]
    for part in range(pieces):
        where = slice(part * rows, part * rows + rows)
        if last and part == 0:
            out_refs[0][...] = dk[where, :] * SCALE
            out_refs[1][...] = dv[where, :]
        else:
            ref = out_refs[part + 1 if last else part]
            ref[:, :HD] = (dk[where, :] * SCALE).astype(bf16)
            ref[:, HD:] = dv[where, :].astype(bf16)


def backward(at, q_blocks, g_blocks, kv_pieces, starts, before=None):
    blocks = len(q_blocks)
    pieces = len(kv_pieces)
    wide = q_blocks[0].shape[1]
    rows = kv_pieces[0].shape[0]
    keys = pieces * rows
    last = before is not None
    packed = ((rows, 2 * HD), bf16)
    if last:
        outs = [((HD, wide), bf16)] * blocks + [((rows, HD), f32)] * 2 + [packed] * (pieces - 1)
    else:
        outs = [((blocks, HD, wide), f32)] + [packed] * pieces
    scratch = [
        pltpu.VMEM((keys, 2 * HD), bf16),
        pltpu.VMEM((keys, 2 * HD), bf16),
        pltpu.VMEM((HD, keys), bf16),
        pltpu.VMEM((blocks, 2 * HD, wide), bf16),
        pltpu.VMEM((blocks, 2 * HD, wide), bf16),
        pltpu.VMEM((keys, HD), f32),
        pltpu.VMEM((keys, HD), f32),
    ]
    if last:
        scratch.append(pltpu.VMEM((blocks, HD, wide), bf16))
    args = [*q_blocks, *g_blocks, *kv_pieces] + ([before] if last else [])
    out = call(
        functools.partial(
            backward_kernel, blocks=blocks, starts=starts, first=not last, last=last
        ),
        [SMEM] + [VMEM] * len(args),
        outs,
        scratch,
        work=2 * 10**10,
    )(at, *args)
    count = blocks if last else 1
    return (out[:blocks] if last else out[0]), out[count:]


def unrotate(x, c, s):
    return x * c - pltpu.roll(x, HD // 2, 1) * s


def query_grad_kernel(z, cf, sf, ct, st, d0, d1, d2, d3, out):
    c, s = query_angles(cf, sf, ct, st, out.shape[0] // FTOK)
    for which in range(2):

        @pl.when(z[0] == which)
        def _():
            for head, one, two in ((which, d0, d1), (1 - which, d2, d3)):
                total = one[...].astype(f32) + two[...].astype(f32)
                out[:, head * HD : head * HD + HD] = unrotate(total.T, c, s)


def key_grad_kernel(z, cf, sf, ct, st, dk, dv, far, par, far_par, dk_out, dv_out):
    c, s = key_angles(cf, sf, ct, st, dk.shape[0] // FTOK)
    for which in range(2):

        @pl.when(z[0] == which)
        def _():
            cols = slice(which * HD, which * HD + HD)
            dk_out[:, cols] = unrotate(dk[...] + far[:, :HD].astype(f32), c, s)
            dv_out[:, cols] = dv[...] + far[:, HD:].astype(f32)
            cols = slice(HD - which * HD, 2 * HD - which * HD)
            total = par[...].astype(f32) + far_par[...].astype(f32)
            dk_out[:, cols] = unrotate(total[:, :HD], c, s)
            dv_out[:, cols] = total[:, HD:]


def ctx_swap(turn, flip):
    def target(x, z):
        x = (x, x ^ 1, 3 - x)[turn]
        return x * 2 + (z ^ flip)

    return [(x * 2 + z, target(x, z)) for x in range(4) for z in range(2)]


def send_ctx(array, turn, flip):
    return lax.ppermute(array, "ctx", ctx_swap(turn, flip))


def frame_xor(mask):
    return [(i, i ^ mask) for i in range(16)]


QUAD_MASKS = (0, 1, 8, 9)
Y_MASKS = (0, 2, 4, 6)


def send_frame(array, mask):
    return array if mask == 0 else lax.ppermute(array, "frame", frame_xor(mask))


def exchange(blocks):
    same, near, other, near_other = blocks
    return [same, send_ctx(near, 1, 0), send_ctx(other, 0, 1), send_ctx(near_other, 1, 1)]


def tables(position):
    half_width = HD // 2
    frequency = jnp.exp(-math.log(10000.0) * jnp.arange(half_width, dtype=f32) / half_width)
    frequency = jnp.concatenate([frequency, frequency])
    angle = position.astype(f32)[:, None] * frequency[None, :]
    return jnp.cos(angle), jnp.sin(angle)


def shards(
    queries,
    keys,
    values,
    query_frames,
    frame_counts,
    clip_of_frame,
    in_proj,
    mlp_up,
    mlp_down,
    reward_head,
):
    ctx_index = lax.axis_index("ctx")
    frame_index = lax.axis_index("frame")
    query_rows = queries.shape[0]
    key_rows = keys.shape[0]
    frame_slots = query_frames.shape[0]
    key_frames = frame_counts.shape[0]
    in_frame = jnp.arange(FTOK, dtype=jnp.int32)
    key_slots = key_rows // FTOK
    frames = jnp.concatenate(
        [query_frames, ctx_index * key_slots + jnp.arange(key_slots, dtype=jnp.int32)]
    )
    cf, sf = tables(frames * FTOK)
    ct, st = tables(in_frame)
    z = (ctx_index % 2).reshape(1).astype(jnp.int32)
    starts = jnp.stack([ctx_index, ctx_index ^ 1, 6 - ctx_index + 2 * z[0], 7 - ctx_index])
    at = jnp.concatenate([jnp.sum(frame_counts).reshape(1), starts * key_rows]).astype(jnp.int32)

    packed_rows = ((key_rows, 2 * HD), bf16)
    kv_own, kv_send = call(
        rotate_key_kernel,
        [SMEM] + [VMEM] * 6,
        [packed_rows] * 2,
    )(z, keys, values, cf, sf, ct, st)
    kv_far = send_ctx(kv_own, 2, 0)
    qs, qo = call(
        rotate_query_kernel,
        [SMEM] + [VMEM] * 5,
        [((HD, query_rows), bf16)] * 2,
    )(z, queries, cf, sf, ct, st)
    q_blocks = exchange((qs, qs, qo, qo))
    kv_send, _ = lax.optimization_barrier((kv_send, qs))
    kv_par = send_ctx(kv_send, 0, 1)
    kv_far_par = send_ctx(kv_send, 2, 1)

    slot_index = jnp.arange(frame_slots, dtype=jnp.int32)
    same_clip = clip_of_frame[:, None] == clip_of_frame[None, :]
    earlier = slot_index[None, :] < slot_index[:, None]
    rank = jnp.sum(jnp.logical_and(same_clip, earlier), axis=1).astype(jnp.int32)
    away = clip_of_frame ^ frame_index
    quad = (away >> 3) * 2 + (away & 1)
    slot_place = (quad * 4 + ((away >> 1) & 3)) * CLIP + rank
    place = (slot_place[:, None] * FTOK + in_frame[None, :]).reshape(1, query_rows)
    frame_match = query_frames[:, None] == jnp.arange(key_frames, dtype=jnp.int32)[None, :]
    slot_counts = jnp.sum(jnp.where(frame_match, frame_counts[None, :], 0), axis=1)
    mine = slot_place[None, :] == jnp.arange(CLIP, dtype=jnp.int32)[:, None]
    my_counts = jnp.sum(jnp.where(mine, slot_counts[None, :], 0), axis=1)
    clip_live = (in_frame[None, :] < my_counts[:, None]).reshape(-1).astype(f32)
    clip_live = jnp.broadcast_to(clip_live[:, None], (CLIP * FTOK, HD))

    before = forward(at, q_blocks, (kv_own, kv_far), (1, 3))
    in_proj, _ = lax.optimization_barrier((in_proj, before[1]))
    near = send_frame(in_proj, 8)
    partial = forward(at, q_blocks, (kv_par, kv_far_par), (2, 4), before)
    in_proj, near_late, _ = lax.optimization_barrier((in_proj, near, partial[0]))
    weights = (in_proj, send_frame(in_proj, 1), near_late, send_frame(near_late, 1))
    partial = exchange(partial)
    width = queries.shape[1]
    quarter = query_rows // 4
    out_t, logs, *chunks = call(
        combine_kernel,
        [SMEM] + [VMEM] * 5,
        [((width, query_rows), bf16), ((2, 8, query_rows), f32)] + [((quarter, width), bf16)] * 4,
    )(z, place, *partial)
    chunks = [send_frame(chunk, mask) for chunk, mask in zip(chunks, QUAD_MASKS)]
    vision = in_proj.shape[1]
    clip_rows = CLIP * FTOK
    inputs = call(
        project_kernel,
        [VMEM] * 8,
        [((clip_rows, vision), f32)] + [((clip_rows, vision), bf16)] * 3,
    )(*chunks, *weights)
    inputs = [send_frame(x, mask) for x, mask in zip(inputs, Y_MASKS)]
    any_spec = pl.BlockSpec(memory_space=pl.ANY)
    input_grad, reward = call(
        reward_kernel,
        [VMEM] * 6 + [any_spec] * 2,
        [((clip_rows, vision), bf16), ((8, HD), f32)],
        [
            pltpu.VMEM(mlp_up.shape, bf16),
            pltpu.VMEM(mlp_down.shape, bf16),
            pltpu.SemaphoreType.DMA((2,)),
        ],
    )(*inputs, clip_live, reward_head.reshape(1, -1), mlp_up, mlp_down)
    grads = [send_frame(input_grad, mask) for mask in Y_MASKS]
    grads = call(
        unproject_kernel,
        [VMEM] * 8,
        [((quarter, width), bf16)] * 4,
        [pltpu.VMEM((quarter, vision), bf16)],
    )(*grads, *weights)
    grads = [send_frame(grad, mask) for grad, mask in zip(grads, QUAD_MASKS)]
    packed = (HD + EXTRA, query_rows)
    gs, go = call(
        ungroup_kernel,
        [SMEM] + [VMEM] * 7,
        [(packed, bf16)] * 2,
        [pltpu.VMEM((query_rows, width), bf16)],
    )(z, place, *grads, out_t, logs)
    g_blocks = exchange((gs, gs, go, go))
    dq, (d_par, d_far_par) = backward(at, q_blocks, g_blocks, (kv_par, kv_far_par), (2, 4))
    d_par = send_ctx(d_par, 0, 1)
    d_far_par = send_ctx(d_far_par, 2, 1)
    dq, (dk_own, dv_own, d_far) = backward(
        at, q_blocks, g_blocks, (kv_own, kv_far), (1, 3), dq
    )
    d_far = send_ctx(d_far, 2, 0)
    dq = exchange(dq)
    (query_grad,) = call(
        query_grad_kernel,
        [SMEM] + [VMEM] * 8,
        [((query_rows, width), f32)],
    )(z, cf, sf, ct, st, *dq)
    key_grad, value_grad = call(
        key_grad_kernel,
        [SMEM] + [VMEM] * 9,
        [((key_rows, width), f32)] * 2,
    )(z, cf, sf, ct, st, dk_own, dv_own, d_far, d_par, d_far_par)
    return query_grad, key_grad, value_grad, reward[0, :1]


def solution(mesh):
    return jax.shard_map(
        shards,
        mesh=mesh,
        in_specs=(
            P("ctx", "frame"),
            P("ctx", "frame"),
            P("ctx", "frame"),
            P("ctx"),
            P(),
            P("ctx"),
            P("frame", None),
            P(),
            P(),
            P(),
        ),
        out_specs=(P("ctx", "frame"), P("ctx", "frame"), P("ctx", "frame"), P(("ctx", "frame"))),
        check_vma=False,
    )
```

```python
import functools
import math

import jax
import jax.numpy as jnp
from jax import lax
from jax.experimental import pallas as pl
from jax.experimental.pallas import tpu as pltpu
from jax.sharding import PartitionSpec as P

HD = 128
FTOK = 16
CLIP = 2
EPSILON = 1e-05
SCALE = 1.0 / math.sqrt(HD)
EXP2_SCALE = SCALE * math.log2(math.e)
DEAD = -1e30
EXTRA = 16
CHUNK = 512


f32 = jnp.float32
bf16 = jnp.bfloat16

NN = (((1,), (0,)), ((), ()))
NT = (((1,), (1,)), ((), ()))
TN = (((0,), (0,)), ((), ()))

VMEM = pl.BlockSpec(memory_space=pltpu.VMEM)
SMEM = pl.BlockSpec(memory_space=pltpu.SMEM)


def dot(left, right, dims):
    return lax.dot_general(left, right, dims, preferred_element_type=f32)


def call(kernel, in_specs, outs, scratch=(), work=0):
    return pl.pallas_call(
        kernel,
        cost_estimate=pl.CostEstimate(flops=work, transcendentals=0, bytes_accessed=1 << 20),
        out_shape=[jax.ShapeDtypeStruct(shape, dtype) for shape, dtype in outs],
        in_specs=in_specs,
        out_specs=[VMEM] * len(outs),
        scratch_shapes=list(scratch),
        compiler_params=pltpu.CompilerParams(vmem_limit_bytes=24 * 1024 * 1024),
    )


def split3(x):
    high = x.astype(bf16).astype(f32)
    rest = x - high
    middle = rest.astype(bf16).astype(f32)
    low = (rest - middle).astype(bf16).astype(f32)
    return high, middle, low


def angles(frame):
    lane = lax.broadcasted_iota(jnp.int32, (1, HD), 1).astype(f32)
    half_width = HD // 2
    lane = jnp.where(lane < half_width, lane, lane - half_width)
    angle = frame * jnp.exp(lane * (-math.log(10000.0) / half_width))
    return jnp.cos(angle), jnp.sin(angle)


def spread_angles(table):
    slots = table.shape[1] - FTOK
    cf, sf = table[0, :slots, :], table[1, :slots, :]
    ct, st = table[0, slots:, :], table[1, slots:, :]
    c = cf[:, None, :] * ct[None] - sf[:, None, :] * st[None]
    s = sf[:, None, :] * ct[None] + cf[:, None, :] * st[None]
    rows = slots * FTOK
    lane = lax.broadcasted_iota(jnp.int32, (rows, HD), 1)
    return c.reshape(rows, HD), jnp.where(lane < HD // 2, -1.0, 1.0) * s.reshape(rows, HD)


def fill_table(table, frames):
    slots = table.shape[1] - FTOK
    table[0, :slots, :], table[1, :slots, :] = angles(frames * FTOK)
    token = lax.broadcasted_iota(jnp.int32, (FTOK, HD), 0).astype(f32)
    table[0, slots:, :], table[1, slots:, :] = angles(token)


def rotate_query_kernel(ctx, frames, x, own, other, table, places):
    slots = frames.shape[0]
    for i in range(slots):
        places[i : i + 1, :] = jnp.full((1, HD), frames[i].astype(f32))
    fill_table(table, places[...])
    c, s = spread_angles(table)
    for which in range(2):

        @pl.when(ctx[0] % 2 == which)
        def _():
            for side, out in ((which, own), (1 - which, other)):
                head = x[:, side * HD : side * HD + HD].astype(f32)
                turned = head * c + pltpu.roll(head, HD // 2, 1) * s
                out[...] = turned.T.astype(bf16)


def rotate_key_kernel(ctx, x, v, own, other, table):
    slots = x.shape[0] // FTOK
    row = lax.broadcasted_iota(jnp.int32, (slots, HD), 0)
    fill_table(table, (row + ctx[0] * slots).astype(f32))
    c, s = spread_angles(table)
    for which in range(2):

        @pl.when(ctx[0] % 2 == which)
        def _():
            for side, out in ((which, own), (1 - which, other)):
                cols = slice(side * HD, side * HD + HD)
                head = x[:, cols].astype(f32)
                turned = head * c + pltpu.roll(head, HD // 2, 1) * s
                out[:, :HD] = turned.astype(bf16)
                out[:, HD:] = v[:, cols]


def fill_keys(ctx, counts, starts, kv_refs, kaug):
    rows = kv_refs[0].shape[0]
    lane = lax.broadcasted_iota(jnp.int32, (rows, HD), 1)
    row = lax.broadcasted_iota(jnp.int32, (rows, HD), 0)
    ones = jnp.where((lane >= 3) & (lane < 6), 1.0, 0.0)
    live = jnp.sum(jnp.sum(counts[...].astype(f32), axis=0, keepdims=True), axis=1, keepdims=True)
    me = ctx[0]
    owners = (me, me ^ 1, 6 - me + 2 * (me % 2), 7 - me)
    for part, ref in enumerate(kv_refs):
        place = (row + owners[starts[part]] * rows).astype(f32)
        bias = jnp.where(place < live, 0.0, DEAD)
        kaug[part * rows : part * rows + rows, :HD] = ref[:, :HD]
        kaug[part * rows : part * rows + rows, HD:] = jnp.where(lane == 6, bias, ones).astype(bf16)


def forward_kernel(ctx, counts, *refs, blocks, starts, first):
    refs = list(refs)

    def take(count):
        taken = refs[:count]
        del refs[:count]
        return taken

    pieces = len(starts)
    q_refs = take(blocks)
    kv_refs = take(pieces)
    if not first:
        acc_in, stat_in = take(2)
    if first:
        acc_out, stat_out = take(2)
    else:
        out_refs = take(blocks)
    kaug, v_t, q_all, *scores = take(5)
    if not first:
        (out_all,) = take(1)
    rows = kv_refs[0].shape[0]
    keys = pieces * rows
    wide = q_refs[0].shape[1]
    fill_keys(ctx, counts, starts, kv_refs, kaug)
    for part, ref in enumerate(kv_refs):
        v_t[:, part * rows : part * rows + rows] = ref[:, HD:].astype(f32).T.astype(bf16)
    sub = lax.broadcasted_iota(jnp.int32, (HD, wide), 0)
    tail = jnp.where(sub == 6, 1.0, 0.0).astype(bf16)
    for i in range(blocks):
        q_all[i, :HD, :] = q_refs[i][...]
        q_all[i, HD:, :] = tail
    spans = [slice(j * CHUNK, j * CHUNK + CHUNK) for j in range(keys // CHUNK)]

    def score(i, slot, span, top):
        s = dot(kaug[span, :], q_all[i], NN)
        scores[slot][span, :] = s
        return jnp.maximum(top, jnp.max(s, axis=0, keepdims=True))

    def start(i):
        return jnp.full((1, wide), -jnp.inf, f32) if first else stat_in[i, 0:1, :]

    def block(i, slot, top, follow):
        if first:
            total = jnp.zeros((1, wide), f32)
            acc = jnp.zeros((HD, wide), f32)
        else:
            shrink = jnp.exp2((stat_in[i, 0:1, :] - top) * EXP2_SCALE)
            total = stat_in[i, 1:2, :] * shrink
            acc = acc_in[i] * shrink
        following = start(follow)
        for span in spans:
            following = score(follow, 1 - slot, span, following)
            p = jnp.exp2((scores[slot][span, :] - top) * EXP2_SCALE)
            total = total + jnp.sum(p, axis=0, keepdims=True)
            acc = acc + dot(v_t[:, span], p.astype(bf16), NN)
        if first:
            acc_out[i] = acc
            which = lax.broadcasted_iota(jnp.int32, (8, wide), 0)
            stat_out[i] = jnp.where(which == 0, top, total)
        else:
            out_all[i, :HD, :] = (acc / total).astype(bf16)
            high, middle, low = split3(top + jnp.log(total) * (1.0 / SCALE))
            which = lax.broadcasted_iota(jnp.int32, (EXTRA, wide), 0)
            rest = jnp.where(which == 1, middle, jnp.where(which == 2, low, 0.0))
            out_all[i, HD:, :] = jnp.where(which == 0, high, rest).astype(bf16)
        return following

    top = start(0)
    for span in spans:
        top = score(0, 0, span, top)

    def pair(t, top):
        middle = block(2 * t, 0, top, 2 * t + 1)
        return block(2 * t + 1, 1, middle, jnp.minimum(2 * t + 2, blocks - 1))

    lax.fori_loop(0, blocks // 2, pair, top)
    if not first:
        for i in range(blocks):
            out_refs[i][...] = out_all[i]


def forward(ctx, counts, q_blocks, kv_pieces, starts, before=None):
    blocks = len(q_blocks)
    wide = q_blocks[0].shape[1]
    keys = len(kv_pieces) * kv_pieces[0].shape[0]
    first = before is None
    if first:
        outs = [((blocks, HD, wide), f32), ((blocks, 8, wide), f32)]
    else:
        outs = [((HD + EXTRA, wide), bf16)] * blocks
    args = [*q_blocks, *kv_pieces] + ([] if first else list(before))
    return call(
        functools.partial(forward_kernel, blocks=blocks, starts=starts, first=first),
        [SMEM] + [VMEM] * (len(args) + 1),
        outs,
        [
            pltpu.VMEM((keys, 2 * HD), bf16),
            pltpu.VMEM((HD, keys), bf16),
            pltpu.VMEM((blocks, 2 * HD, wide), bf16),
            pltpu.VMEM((keys, wide), f32),
            pltpu.VMEM((keys, wide), f32),
        ]
        + ([] if first else [pltpu.VMEM((blocks, HD + EXTRA, wide), bf16)]),
        work=10**10,
    )(ctx, counts, *args)


def one_hot(place):
    rows = place.shape[1]
    row = lax.broadcasted_iota(jnp.int32, (rows, rows), 0)
    return jnp.where(row == place[...], 1.0, 0.0).astype(bf16)


def combine_kernel(ctx, place, *refs):
    partial, (out_t, logs, c0, c1, c2, c3) = refs[:4], refs[4:]
    wide = partial[0].shape[1]
    for side in range(2):
        sums = []
        for ref in partial[2 * side : 2 * side + 2]:
            tail = ref[HD:, :].astype(f32)
            sums.append(tail[0:1] + tail[1:2] + tail[2:3])
        top = functools.reduce(jnp.maximum, sums)
        weight = [jnp.exp2((s - top) * EXP2_SCALE) for s in sums]
        total = sum(weight)
        acc = jnp.zeros((HD, wide), f32)
        for w, ref in zip(weight, partial[2 * side : 2 * side + 2]):
            acc = acc + (w / total) * ref[:HD, :].astype(f32)
        logs[side, :, :] = jnp.broadcast_to(top + jnp.log(total) * (1.0 / SCALE), (8, wide))
        head = ctx[0] % 2 if side == 0 else 1 - ctx[0] % 2
        out_t[pl.ds(pl.multiple_of(head * HD, HD), HD), :] = acc.astype(bf16)
    grouped = dot(one_hot(place), out_t[...], NT).astype(bf16)
    quarter = wide // 4
    for i, ref in enumerate((c0, c1, c2, c3)):
        ref[...] = grouped[i * quarter : i * quarter + quarter]


def project_kernel(o0, o1, o2, o3, w0, w1, w2, w3, x0, x1, x2, x3):
    total = None
    for o, w in ((o0, w0), (o1, w1), (o2, w2), (o3, w3)):
        term = dot(o[...], w[...], NN)
        total = term if total is None else total + term
    rows = x0.shape[0]
    for i, ref in enumerate((x0, x1, x2, x3)):
        ref[...] = total[i * rows : i * rows + rows].astype(ref.dtype)


def unproject_kernel(g0, g1, g2, g3, w0, w1, w2, w3, d0, d1, d2, d3, g):
    rows = g0.shape[0]
    for i, ref in enumerate((g0, g1, g2, g3)):
        g[i * rows : i * rows + rows, :] = ref[...]
    for w, d in ((w0, d0), (w1, d1), (w2, d2), (w3, d3)):
        d[...] = dot(g[...], w[...], NT).astype(bf16)


def center(x):
    mean = jnp.mean(x, axis=1, keepdims=True)
    shifted = x - mean
    rate = lax.rsqrt(jnp.mean(shifted * shifted, axis=1, keepdims=True) + EPSILON)
    return shifted * rate, rate


def center_grad(grad, normed, rate):
    return rate * (
        grad
        - jnp.mean(grad, axis=1, keepdims=True)
        - normed * jnp.mean(grad * normed, axis=1, keepdims=True)
    )


def reward_kernel(counts, x0, x1, x2, x3, head, up, down, grad_out, reward_out, slopes):
    steps, _, part = slopes.shape
    vision = up.shape[0]

    def piece(j):
        return pl.ds(pl.multiple_of(j * part, part), part)

    rows = x0.shape[0]

    def live(shape, axis):
        row = lax.broadcasted_iota(jnp.int32, shape, axis)
        left = jnp.where(row < FTOK, counts[0], counts[1] + FTOK)
        return jnp.where(row < left, 1.0, 0.0)

    x = x0[...].astype(f32) + x1[...].astype(f32) + x2[...].astype(f32) + x3[...].astype(f32)
    normed, rate = center(x)
    low_normed = normed.astype(bf16)
    c0 = math.sqrt(2.0 / math.pi)
    c1 = 0.044715

    def upward(j, hidden):
        before = dot(low_normed, up[:, piece(j)], NN)
        square = before * before
        tanh = jnp.tanh(c0 * before * (1.0 + c1 * square))
        half = 0.5 * (1.0 + tanh)
        slope = half + 0.5 * before * (1.0 - tanh * tanh) * (c0 * (1.0 + 3.0 * c1 * square))
        slopes[j] = slope
        return hidden + dot((before * half).astype(bf16), down[piece(j), :], NN)

    hidden = lax.fori_loop(0, steps, upward, jnp.zeros((rows, vision), f32))
    alive = live((rows, 1), 0)
    count = jnp.sum(alive, axis=0, keepdims=True)
    pooled = jnp.sum(hidden * alive, axis=0, keepdims=True) / count
    pooled_normed, pooled_rate = center(pooled)
    reward = count * jnp.sum(pooled_normed * head[...], axis=1, keepdims=True)
    reward_out[...] = jnp.broadcast_to(reward, reward_out.shape)
    pooled_grad = center_grad(count * head[...], pooled_normed, pooled_rate) / count
    high, middle, low = split3(pooled_grad)
    which = lax.broadcasted_iota(jnp.int32, (EXTRA, vision), 0)
    pieces = jnp.where(which == 0, high, jnp.where(which == 1, middle, jnp.where(which == 2, low, 0.0)))
    pieces_b = pieces.astype(bf16)
    alive_t = live((1, rows), 1)

    def downward(j, normed_grad):
        spread = jnp.sum(dot(pieces_b, down[piece(j), :], NT), axis=0, keepdims=True)
        before_grad = (spread * slopes[j] * alive).astype(bf16)
        return normed_grad + dot(before_grad, up[:, piece(j)], NT)

    normed_grad = lax.fori_loop(0, steps, downward, jnp.zeros((rows, vision), f32))
    grad_out[...] = center_grad(normed_grad, normed, rate).astype(bf16)


def reward_call(counts, inputs, head, mlp_up, mlp_down):
    vision, hidden = mlp_up.shape
    steps = 8
    part = hidden // steps
    rows = inputs[0].shape[0]
    return call(
        reward_kernel,
        [SMEM] + [VMEM] * 7,
        [((rows, vision), bf16), ((8, HD), f32)],
        [
            pltpu.VMEM((steps, rows, part), f32),
        ],
    )(counts, *inputs, head.reshape(1, -1), mlp_up, mlp_down)


def ungroup_kernel(ctx, place, d0, d1, d2, d3, out_t, logs, ps, po, grad):
    quarter = d0.shape[0]
    for i, ref in enumerate((d0, d1, d2, d3)):
        grad[i * quarter : i * quarter + quarter, :] = ref[...]
    wide = place.shape[1]
    grad_t = dot(grad[...], one_hot(place), TN)
    product = grad_t * out_t[...].astype(f32)
    which = lax.broadcasted_iota(jnp.int32, (EXTRA, wide), 0)
    for head in range(2):
        delta = jnp.sum(product[head * HD : head * HD + HD], axis=0, keepdims=True)
        for side, ref in enumerate((ps, po)):

            @pl.when(head == (ctx[0] % 2 if side == 0 else 1 - ctx[0] % 2))
            def _():
                ref[:HD, :] = grad_t[head * HD : head * HD + HD].astype(bf16)
                rows = split3(delta) + split3(-logs[side, 0:1, :])
                tail = jnp.where(which == 6, 1.0, 0.0)
                for i, piece in enumerate(rows):
                    tail = jnp.where(which == i, piece, tail)
                ref[HD:, :] = tail.astype(bf16)


def backward_kernel(ctx, counts, *refs, blocks, starts, first, last):
    refs = list(refs)

    def take(count):
        taken = refs[:count]
        del refs[:count]
        return taken

    pieces = len(starts)
    q_refs = take(blocks)
    g_refs = take(blocks)
    kv_refs = take(pieces)
    if not first:
        (dq_in,) = take(1)
    dq_refs = take(blocks) if last else take(1)
    out_refs = take(pieces + 1) if last else take(pieces)
    kaug, vaug, k_t, q_all, g_all, dk, dv = take(7)
    if last:
        (dq_all,) = take(1)
    rows = kv_refs[0].shape[0]
    keys = pieces * rows
    wide = q_refs[0].shape[1]
    fill_keys(ctx, counts, starts, kv_refs, kaug)
    lane = lax.broadcasted_iota(jnp.int32, (rows, HD), 1)
    minus = jnp.where(lane < 3, -1.0, 0.0).astype(bf16)
    for part, ref in enumerate(kv_refs):
        where = slice(part * rows, part * rows + rows)
        vaug[where, :HD] = ref[:, HD:]
        vaug[where, HD:] = minus
        k_t[:, where] = ref[:, :HD].astype(f32).T.astype(bf16)
    dk[...] = jnp.zeros_like(dk)
    dv[...] = jnp.zeros_like(dv)
    blank = jnp.zeros((HD - EXTRA, wide), bf16)
    for i in range(blocks):
        q_all[i, :HD, :] = q_refs[i][...]
        q_all[i, HD : HD + EXTRA, :] = g_refs[i][HD:, :]
        q_all[i, HD + EXTRA :, :] = blank
        g_all[i, : HD + EXTRA, :] = g_refs[i][...]
        g_all[i, HD + EXTRA :, :] = blank

    def block(i, carry):
        query = q_all[i]
        grad = g_all[i]
        acc = jnp.zeros((HD, wide), f32) if first else dq_in[i]
        for j in range(keys // CHUNK):
            part = slice(j * CHUNK, j * CHUNK + CHUNK)
            p = jnp.exp2(dot(kaug[part, :], query, NN) * EXP2_SCALE)
            ds = (p * dot(vaug[part, :], grad, NN)).astype(bf16)
            dv[part, :] += dot(p.astype(bf16), grad[:HD], NT)
            dk[part, :] += dot(ds, query[:HD], NT)
            acc = acc + dot(k_t[:, part], ds, NN)
        if last:
            dq_all[i] = (acc * SCALE).astype(bf16)
        else:
            dq_refs[0][i] = acc
        return carry

    lax.fori_loop(0, blocks, block, 0)
    if last:
        for i in range(blocks):
            dq_refs[i][...] = dq_all[i]
    for part in range(pieces):
        where = slice(part * rows, part * rows + rows)
        if last and part == 0:
            out_refs[0][...] = dk[where, :] * SCALE
            out_refs[1][...] = dv[where, :]
        else:
            ref = out_refs[part + 1 if last else part]
            ref[:, :HD] = (dk[where, :] * SCALE).astype(bf16)
            ref[:, HD:] = dv[where, :].astype(bf16)


def backward(ctx, counts, q_blocks, g_blocks, kv_pieces, starts, before=None):
    blocks = len(q_blocks)
    pieces = len(kv_pieces)
    wide = q_blocks[0].shape[1]
    rows = kv_pieces[0].shape[0]
    keys = pieces * rows
    last = before is not None
    packed = ((rows, 2 * HD), bf16)
    if last:
        outs = [((HD, wide), bf16)] * blocks + [((rows, HD), f32)] * 2 + [packed] * (pieces - 1)
    else:
        outs = [((blocks, HD, wide), f32)] + [packed] * pieces
    scratch = [
        pltpu.VMEM((keys, 2 * HD), bf16),
        pltpu.VMEM((keys, 2 * HD), bf16),
        pltpu.VMEM((HD, keys), bf16),
        pltpu.VMEM((blocks, 2 * HD, wide), bf16),
        pltpu.VMEM((blocks, 2 * HD, wide), bf16),
        pltpu.VMEM((keys, HD), f32),
        pltpu.VMEM((keys, HD), f32),
    ]
    if last:
        scratch.append(pltpu.VMEM((blocks, HD, wide), bf16))
    args = [*q_blocks, *g_blocks, *kv_pieces] + ([before] if last else [])
    out = call(
        functools.partial(
            backward_kernel, blocks=blocks, starts=starts, first=not last, last=last
        ),
        [SMEM] + [VMEM] * (len(args) + 1),
        outs,
        scratch,
        work=2 * 10**10,
    )(ctx, counts, *args)
    count = blocks if last else 1
    return (out[:blocks] if last else out[0]), out[count:]


def unrotate(x, c, s):
    return x * c - pltpu.roll(x, HD // 2, 1) * s


def query_grad_kernel(ctx, table, d0, d1, d2, d3, out):
    c, s = spread_angles(table)
    for which in range(2):

        @pl.when(ctx[0] % 2 == which)
        def _():
            for head, one, two in ((which, d0, d1), (1 - which, d2, d3)):
                total = one[...].astype(f32) + two[...].astype(f32)
                out[:, head * HD : head * HD + HD] = unrotate(total.T, c, s)


def key_grad_kernel(ctx, table, dk, dv, far, par, far_par, dk_out, dv_out):
    c, s = spread_angles(table)
    for which in range(2):

        @pl.when(ctx[0] % 2 == which)
        def _():
            cols = slice(which * HD, which * HD + HD)
            dk_out[:, cols] = unrotate(dk[...] + far[:, :HD].astype(f32), c, s)
            dv_out[:, cols] = dv[...] + far[:, HD:].astype(f32)
            cols = slice(HD - which * HD, 2 * HD - which * HD)
            total = par[...].astype(f32) + far_par[...].astype(f32)
            dk_out[:, cols] = unrotate(total[:, :HD], c, s)
            dv_out[:, cols] = total[:, HD:]


def ctx_swap(turn, flip):
    def target(x, z):
        x = (x, x ^ 1, 3 - x)[turn]
        return x * 2 + (z ^ flip)

    return [(x * 2 + z, target(x, z)) for x in range(4) for z in range(2)]


def send_ctx(array, turn, flip):
    return lax.ppermute(array, "ctx", ctx_swap(turn, flip))


def frame_xor(mask):
    return [(i, i ^ mask) for i in range(16)]


QUAD_MASKS = (0, 1, 8, 9)
Y_MASKS = (0, 2, 4, 6)


def send_frame(array, mask):
    return array if mask == 0 else lax.ppermute(array, "frame", frame_xor(mask))


def exchange(blocks):
    same, near, other, near_other = blocks
    return [same, send_ctx(near, 1, 0), send_ctx(other, 0, 1), send_ctx(near_other, 1, 1)]


def shards(
    queries,
    keys,
    values,
    query_frames,
    frame_counts,
    clip_of_frame,
    in_proj,
    mlp_up,
    mlp_down,
    reward_head,
):
    ctx_index = lax.axis_index("ctx")
    frame_index = lax.axis_index("frame")
    query_rows = queries.shape[0]
    key_rows = keys.shape[0]
    frame_slots = query_frames.shape[0]
    key_frames = frame_counts.shape[0]
    in_frame = jnp.arange(FTOK, dtype=jnp.int32)
    ctx = ctx_index.reshape(1).astype(jnp.int32)
    counts = frame_counts.reshape(-1, HD)
    packed_rows = ((key_rows, 2 * HD), bf16)
    key_table = (2, key_rows // FTOK + FTOK, HD)
    kv_own, kv_send, key_table = call(
        rotate_key_kernel,
        [SMEM] + [VMEM] * 2,
        [packed_rows] * 2 + [(key_table, f32)],
    )(ctx, keys, values)
    kv_far = send_ctx(kv_own, 2, 0)
    qs, qo, query_table = call(
        rotate_query_kernel,
        [SMEM] * 2 + [VMEM],
        [((HD, query_rows), bf16)] * 2 + [((2, frame_slots + FTOK, HD), f32)],
        [pltpu.VMEM((frame_slots, HD), f32)],
    )(ctx, query_frames, queries)
    q_blocks = exchange((qs, qs, qo, qo))
    kv_send, _ = lax.optimization_barrier((kv_send, qs))
    kv_par = send_ctx(kv_send, 0, 1)
    kv_far_par = send_ctx(kv_send, 2, 1)

    slot_index = jnp.arange(frame_slots, dtype=jnp.int32)
    same_clip = clip_of_frame[:, None] == clip_of_frame[None, :]
    earlier = slot_index[None, :] < slot_index[:, None]
    rank = jnp.sum(jnp.logical_and(same_clip, earlier), axis=1).astype(jnp.int32)
    away = clip_of_frame ^ frame_index
    quad = (away >> 3) * 2 + (away & 1)
    slot_place = (quad * 4 + ((away >> 1) & 3)) * CLIP + rank
    place = (slot_place[:, None] * FTOK + in_frame[None, :]).reshape(1, query_rows)
    frame_match = query_frames[:, None] == jnp.arange(key_frames, dtype=jnp.int32)[None, :]
    slot_counts = jnp.sum(jnp.where(frame_match, frame_counts[None, :], 0), axis=1)
    mine = slot_place[None, :] == jnp.arange(CLIP, dtype=jnp.int32)[:, None]
    my_counts = jnp.sum(jnp.where(mine, slot_counts[None, :], 0), axis=1).astype(jnp.int32)

    before = forward(ctx, counts, q_blocks, (kv_own, kv_far), (0, 2))
    kv_par, kv_far_par, in_proj, _ = lax.optimization_barrier(
        (kv_par, kv_far_par, in_proj, before[1])
    )
    near = send_frame(in_proj, 8)
    partial = forward(ctx, counts, q_blocks, (kv_par, kv_far_par), (1, 3), before)
    in_proj, near_late, _ = lax.optimization_barrier((in_proj, near, partial[0]))
    weights = (in_proj, send_frame(in_proj, 1), near_late, send_frame(near_late, 1))
    partial = exchange(partial)
    width = queries.shape[1]
    quarter = query_rows // 4
    out_t, logs, *chunks = call(
        combine_kernel,
        [SMEM] + [VMEM] * 5,
        [((width, query_rows), bf16), ((2, 8, query_rows), f32)] + [((quarter, width), bf16)] * 4,
    )(ctx, place, *partial)
    chunks = [send_frame(chunk, mask) for chunk, mask in zip(chunks, QUAD_MASKS)]
    vision = in_proj.shape[1]
    clip_rows = CLIP * FTOK
    inputs = call(
        project_kernel,
        [VMEM] * 8,
        [((clip_rows, vision), f32)] + [((clip_rows, vision), bf16)] * 3,
    )(*chunks, *weights)
    inputs = [send_frame(x, mask) for x, mask in zip(inputs, Y_MASKS)]
    input_grad, reward = reward_call(my_counts, inputs, reward_head, mlp_up, mlp_down)
    grads = [send_frame(input_grad, mask) for mask in Y_MASKS]
    grads = call(
        unproject_kernel,
        [VMEM] * 8,
        [((quarter, width), bf16)] * 4,
        [pltpu.VMEM((quarter, vision), bf16)],
    )(*grads, *weights)
    grads = [send_frame(grad, mask) for grad, mask in zip(grads, QUAD_MASKS)]
    packed = (HD + EXTRA, query_rows)
    gs, go = call(
        ungroup_kernel,
        [SMEM] + [VMEM] * 7,
        [(packed, bf16)] * 2,
        [pltpu.VMEM((query_rows, width), bf16)],
    )(ctx, place, *grads, out_t, logs)
    g_blocks = exchange((gs, gs, go, go))
    dq, (d_par, d_far_par) = backward(ctx, counts, q_blocks, g_blocks, (kv_par, kv_far_par), (1, 3))
    d_par = send_ctx(d_par, 0, 1)
    d_far_par = send_ctx(d_far_par, 2, 1)
    dq, (dk_own, dv_own, d_far) = backward(
        ctx, counts, q_blocks, g_blocks, (kv_own, kv_far), (0, 2), dq
    )
    d_far = send_ctx(d_far, 2, 0)
    dq = exchange(dq)
    (query_grad,) = call(
        query_grad_kernel,
        [SMEM] + [VMEM] * 5,
        [((query_rows, width), f32)],
    )(ctx, query_table, *dq)
    key_grad, value_grad = call(
        key_grad_kernel,
        [SMEM] + [VMEM] * 6,
        [((key_rows, width), f32)] * 2,
    )(ctx, key_table, dk_own, dv_own, d_far, d_par, d_far_par)
    return query_grad, key_grad, value_grad, reward[0, :1]


def solution(mesh):
    return jax.shard_map(
        shards,
        mesh=mesh,
        in_specs=(
            P("ctx", "frame"),
            P("ctx", "frame"),
            P("ctx", "frame"),
            P("ctx"),
            P(),
            P("ctx"),
            P("frame", None),
            P(),
            P(),
            P(),
        ),
        out_specs=(P("ctx", "frame"), P("ctx", "frame"), P("ctx", "frame"), P(("ctx", "frame"))),
        check_vma=False,
    )
```

```python
import functools
import math

import jax
import jax.numpy as jnp
from jax import lax
from jax.experimental import pallas as pl
from jax.experimental.pallas import tpu as pltpu
from jax.sharding import PartitionSpec as P

HD = 128
FTOK = 16
CLIP = 2
EPSILON = 1e-05
SCALE = 1.0 / math.sqrt(HD)
EXP2_SCALE = SCALE * math.log2(math.e)
DEAD = -1e30
EXTRA = 16
CHUNK = 512


f32 = jnp.float32
bf16 = jnp.bfloat16

NN = (((1,), (0,)), ((), ()))
NT = (((1,), (1,)), ((), ()))
TN = (((0,), (0,)), ((), ()))

VMEM = pl.BlockSpec(memory_space=pltpu.VMEM)
SMEM = pl.BlockSpec(memory_space=pltpu.SMEM)


def dot(left, right, dims):
    return lax.dot_general(left, right, dims, preferred_element_type=f32)


def call(kernel, in_specs, outs, scratch=(), work=0):
    return pl.pallas_call(
        kernel,
        cost_estimate=pl.CostEstimate(flops=work, transcendentals=0, bytes_accessed=1 << 20),
        out_shape=[jax.ShapeDtypeStruct(shape, dtype) for shape, dtype in outs],
        in_specs=in_specs,
        out_specs=[VMEM] * len(outs),
        scratch_shapes=list(scratch),
        compiler_params=pltpu.CompilerParams(vmem_limit_bytes=16 * 1024 * 1024),
    )


def split3(x):
    high = x.astype(bf16).astype(f32)
    rest = x - high
    middle = rest.astype(bf16).astype(f32)
    low = (rest - middle).astype(bf16).astype(f32)
    return high, middle, low


def angles(frame):
    lane = lax.broadcasted_iota(jnp.int32, (1, HD), 1).astype(f32)
    half_width = HD // 2
    lane = jnp.where(lane < half_width, lane, lane - half_width)
    angle = frame * jnp.exp(lane * (-math.log(10000.0) / half_width))
    return jnp.cos(angle), jnp.sin(angle)


def spread_angles(table):
    slots = table.shape[1] - FTOK
    cf, sf = table[0, :slots, :], table[1, :slots, :]
    ct, st = table[0, slots:, :], table[1, slots:, :]
    c = cf[:, None, :] * ct[None] - sf[:, None, :] * st[None]
    s = sf[:, None, :] * ct[None] + cf[:, None, :] * st[None]
    rows = slots * FTOK
    lane = lax.broadcasted_iota(jnp.int32, (rows, HD), 1)
    return c.reshape(rows, HD), jnp.where(lane < HD // 2, -1.0, 1.0) * s.reshape(rows, HD)


def fill_table(table, frames):
    slots = table.shape[1] - FTOK
    table[0, :slots, :], table[1, :slots, :] = angles(frames * FTOK)
    token = lax.broadcasted_iota(jnp.int32, (FTOK, HD), 0).astype(f32)
    table[0, slots:, :], table[1, slots:, :] = angles(token)


def rotate_query_kernel(ctx, frames, x, own, other, table, places):
    slots = frames.shape[0]
    for i in range(slots):
        places[i : i + 1, :] = jnp.full((1, HD), frames[i].astype(f32))
    fill_table(table, places[...])
    c, s = spread_angles(table)
    for which in range(2):

        @pl.when(ctx[0] % 2 == which)
        def _():
            for side, out in ((which, own), (1 - which, other)):
                head = x[:, side * HD : side * HD + HD].astype(f32)
                turned = head * c + pltpu.roll(head, HD // 2, 1) * s
                out[...] = turned.T.astype(bf16)


def rotate_key_kernel(ctx, x, v, own, other, table):
    slots = x.shape[0] // FTOK
    row = lax.broadcasted_iota(jnp.int32, (slots, HD), 0)
    fill_table(table, (row + ctx[0] * slots).astype(f32))
    c, s = spread_angles(table)
    for which in range(2):

        @pl.when(ctx[0] % 2 == which)
        def _():
            for side, out in ((which, own), (1 - which, other)):
                cols = slice(side * HD, side * HD + HD)
                head = x[:, cols].astype(f32)
                turned = head * c + pltpu.roll(head, HD // 2, 1) * s
                out[:, :HD] = turned.astype(bf16)
                out[:, HD:] = v[:, cols]


def fill_keys(ctx, counts, starts, kv_refs, kaug):
    rows = kv_refs[0].shape[0]
    lane = lax.broadcasted_iota(jnp.int32, (rows, HD), 1)
    row = lax.broadcasted_iota(jnp.int32, (rows, HD), 0)
    ones = jnp.where((lane >= 3) & (lane < 6), 1.0, 0.0)
    live = jnp.sum(jnp.sum(counts[...].astype(f32), axis=0, keepdims=True), axis=1, keepdims=True)
    me = ctx[0]
    owners = (me, me ^ 1, 6 - me + 2 * (me % 2), 7 - me)
    for part, ref in enumerate(kv_refs):
        place = (row + owners[starts[part]] * rows).astype(f32)
        bias = jnp.where(place < live, 0.0, DEAD)
        kaug[part * rows : part * rows + rows, :HD] = ref[:, :HD]
        kaug[part * rows : part * rows + rows, HD:] = jnp.where(lane == 6, bias, ones).astype(bf16)


def forward_kernel(ctx, counts, *refs, blocks, starts, first, last, extras):
    refs = list(refs)

    def take(count):
        taken = refs[:count]
        del refs[:count]
        return taken

    pieces = len(starts)
    q_refs = take(blocks)
    kv_refs = take(pieces)
    if not first:
        acc_in, stat_in = take(2)
    take(extras)
    if last:
        out_refs = take(blocks)
    else:
        acc_out, stat_out = take(2)
    kaug, v_t, q_all, *scores = take(5)
    if last:
        (out_all,) = take(1)
    rows = kv_refs[0].shape[0]
    keys = pieces * rows
    wide = q_refs[0].shape[1]
    fill_keys(ctx, counts, starts, kv_refs, kaug)
    for part, ref in enumerate(kv_refs):
        v_t[:, part * rows : part * rows + rows] = ref[:, HD:].astype(f32).T.astype(bf16)
    sub = lax.broadcasted_iota(jnp.int32, (HD, wide), 0)
    tail = jnp.where(sub == 6, 1.0, 0.0).astype(bf16)
    for i in range(blocks):
        q_all[i, :HD, :] = q_refs[i][...]
        q_all[i, HD:, :] = tail
    spans = [slice(j * CHUNK, j * CHUNK + CHUNK) for j in range(keys // CHUNK)]

    def score(i, slot, span, top):
        s = dot(kaug[span, :], q_all[i], NN)
        scores[slot][span, :] = s
        return jnp.maximum(top, jnp.max(s, axis=0, keepdims=True))

    def start(i):
        return jnp.full((1, wide), -jnp.inf, f32) if first else stat_in[i, 0:1, :]

    def block(i, slot, top, follow):
        if first:
            total = jnp.zeros((1, wide), f32)
            acc = jnp.zeros((HD, wide), f32)
        else:
            shrink = jnp.exp2((stat_in[i, 0:1, :] - top) * EXP2_SCALE)
            total = stat_in[i, 1:2, :] * shrink
            acc = acc_in[i] * shrink
        following = start(follow)
        for span in spans:
            following = score(follow, 1 - slot, span, following)
            p = jnp.exp2((scores[slot][span, :] - top) * EXP2_SCALE)
            total = total + jnp.sum(p, axis=0, keepdims=True)
            acc = acc + dot(v_t[:, span], p.astype(bf16), NN)
        if not last:
            acc_out[i] = acc
            which = lax.broadcasted_iota(jnp.int32, (8, wide), 0)
            stat_out[i] = jnp.where(which == 0, top, total)
        else:
            out_all[i, :HD, :] = (acc / total).astype(bf16)
            high, middle, low = split3(top + jnp.log(total) * (1.0 / SCALE))
            which = lax.broadcasted_iota(jnp.int32, (EXTRA, wide), 0)
            rest = jnp.where(which == 1, middle, jnp.where(which == 2, low, 0.0))
            out_all[i, HD:, :] = jnp.where(which == 0, high, rest).astype(bf16)
        return following

    top = start(0)
    for span in spans:
        top = score(0, 0, span, top)

    def pair(t, top):
        middle = block(2 * t, 0, top, 2 * t + 1)
        return block(2 * t + 1, 1, middle, jnp.minimum(2 * t + 2, blocks - 1))

    lax.fori_loop(0, blocks // 2, pair, top)
    if last:
        for i in range(blocks):
            out_refs[i][...] = out_all[i]


def forward(ctx, counts, q_blocks, kv_pieces, starts, before=(), last=False, extras=()):
    blocks = len(q_blocks)
    wide = q_blocks[0].shape[1]
    keys = len(kv_pieces) * kv_pieces[0].shape[0]
    if last:
        outs = [((HD + EXTRA, wide), bf16)] * blocks
    else:
        outs = [((blocks, HD, wide), f32), ((blocks, 8, wide), f32)]
    args = [*q_blocks, *kv_pieces, *before, *extras]
    return call(
        functools.partial(
            forward_kernel,
            blocks=blocks,
            starts=starts,
            first=not before,
            last=last,
            extras=len(extras),
        ),
        [SMEM] + [VMEM] * (len(args) + 1),
        outs,
        [
            pltpu.VMEM((keys, 2 * HD), bf16),
            pltpu.VMEM((HD, keys), bf16),
            pltpu.VMEM((blocks, 2 * HD, wide), bf16),
            pltpu.VMEM((keys, wide), f32),
            pltpu.VMEM((keys, wide), f32),
        ]
        + ([pltpu.VMEM((blocks, HD + EXTRA, wide), bf16)] if last else []),
        work=10**10,
    )(ctx, counts, *args)


def one_hot(place):
    rows = place.shape[1]
    row = lax.broadcasted_iota(jnp.int32, (rows, rows), 0)
    return jnp.where(row == place[...], 1.0, 0.0).astype(bf16)


def combine_kernel(ctx, place, *refs):
    partial, (out_t, logs, c0, c1, c2, c3) = refs[:4], refs[4:]
    wide = partial[0].shape[1]
    for side in range(2):
        sums = []
        for ref in partial[2 * side : 2 * side + 2]:
            tail = ref[HD:, :].astype(f32)
            sums.append(tail[0:1] + tail[1:2] + tail[2:3])
        top = functools.reduce(jnp.maximum, sums)
        weight = [jnp.exp2((s - top) * EXP2_SCALE) for s in sums]
        total = sum(weight)
        acc = jnp.zeros((HD, wide), f32)
        for w, ref in zip(weight, partial[2 * side : 2 * side + 2]):
            acc = acc + (w / total) * ref[:HD, :].astype(f32)
        logs[side, :, :] = jnp.broadcast_to(top + jnp.log(total) * (1.0 / SCALE), (8, wide))
        head = ctx[0] % 2 if side == 0 else 1 - ctx[0] % 2
        out_t[pl.ds(pl.multiple_of(head * HD, HD), HD), :] = acc.astype(bf16)
    grouped = dot(one_hot(place), out_t[...], NT).astype(bf16)
    quarter = wide // 4
    for i, ref in enumerate((c0, c1, c2, c3)):
        ref[...] = grouped[i * quarter : i * quarter + quarter]


def project_kernel(o0, o1, o2, o3, w0, w1, w2, w3, x0, x1, x2, x3):
    total = None
    for o, w in ((o0, w0), (o1, w1), (o2, w2), (o3, w3)):
        term = dot(o[...], w[...], NN)
        total = term if total is None else total + term
    rows = x0.shape[0]
    for i, ref in enumerate((x0, x1, x2, x3)):
        ref[...] = total[i * rows : i * rows + rows].astype(ref.dtype)


def unproject_kernel(g0, g1, g2, g3, w0, w1, w2, w3, d0, d1, d2, d3, g):
    rows = g0.shape[0]
    for i, ref in enumerate((g0, g1, g2, g3)):
        g[i * rows : i * rows + rows, :] = ref[...]
    for w, d in ((w0, d0), (w1, d1), (w2, d2), (w3, d3)):
        d[...] = dot(g[...], w[...], NT).astype(bf16)


def center(x):
    mean = jnp.mean(x, axis=1, keepdims=True)
    shifted = x - mean
    rate = lax.rsqrt(jnp.mean(shifted * shifted, axis=1, keepdims=True) + EPSILON)
    return shifted * rate, rate


def center_grad(grad, normed, rate):
    return rate * (
        grad
        - jnp.mean(grad, axis=1, keepdims=True)
        - normed * jnp.mean(grad * normed, axis=1, keepdims=True)
    )


def reward_kernel(counts, x0, x1, x2, x3, head, up, down, grad_out, reward_out, slopes):
    steps, _, part = slopes.shape
    vision = up.shape[0]

    def piece(j):
        return pl.ds(pl.multiple_of(j * part, part), part)

    rows = x0.shape[0]

    def live(shape, axis):
        row = lax.broadcasted_iota(jnp.int32, shape, axis)
        left = jnp.where(row < FTOK, counts[0], counts[1] + FTOK)
        return jnp.where(row < left, 1.0, 0.0)

    x = x0[...].astype(f32) + x1[...].astype(f32) + x2[...].astype(f32) + x3[...].astype(f32)
    normed, rate = center(x)
    low_normed = normed.astype(bf16)
    c0 = math.sqrt(2.0 / math.pi)
    c1 = 0.044715

    def upward(j, hidden):
        before = dot(low_normed, up[:, piece(j)], NN)
        square = before * before
        tanh = jnp.tanh(c0 * before * (1.0 + c1 * square))
        half = 0.5 * (1.0 + tanh)
        slope = half + 0.5 * before * (1.0 - tanh * tanh) * (c0 * (1.0 + 3.0 * c1 * square))
        slopes[j] = slope
        return hidden + dot((before * half).astype(bf16), down[piece(j), :], NN)

    hidden = lax.fori_loop(0, steps, upward, jnp.zeros((rows, vision), f32))
    alive = live((rows, 1), 0)
    count = jnp.sum(alive, axis=0, keepdims=True)
    pooled = jnp.sum(hidden * alive, axis=0, keepdims=True) / count
    pooled_normed, pooled_rate = center(pooled)
    reward = count * jnp.sum(pooled_normed * head[...], axis=1, keepdims=True)
    reward_out[...] = jnp.broadcast_to(reward, reward_out.shape)
    pooled_grad = center_grad(count * head[...], pooled_normed, pooled_rate) / count
    high, middle, low = split3(pooled_grad)
    which = lax.broadcasted_iota(jnp.int32, (EXTRA, vision), 0)
    pieces = jnp.where(which == 0, high, jnp.where(which == 1, middle, jnp.where(which == 2, low, 0.0)))
    pieces_b = pieces.astype(bf16)
    alive_t = live((1, rows), 1)

    def downward(j, normed_grad):
        spread = jnp.sum(dot(pieces_b, down[piece(j), :], NT), axis=0, keepdims=True)
        before_grad = (spread * slopes[j] * alive).astype(bf16)
        return normed_grad + dot(before_grad, up[:, piece(j)], NT)

    normed_grad = lax.fori_loop(0, steps, downward, jnp.zeros((rows, vision), f32))
    grad_out[...] = center_grad(normed_grad, normed, rate).astype(bf16)


def reward_call(counts, inputs, head, mlp_up, mlp_down):
    vision, hidden = mlp_up.shape
    steps = 8
    part = hidden // steps
    rows = inputs[0].shape[0]
    return call(
        reward_kernel,
        [SMEM] + [VMEM] * 7,
        [((rows, vision), bf16), ((8, HD), f32)],
        [
            pltpu.VMEM((steps, rows, part), f32),
        ],
    )(counts, *inputs, head.reshape(1, -1), mlp_up, mlp_down)


def ungroup_kernel(ctx, place, d0, d1, d2, d3, out_t, logs, ps, po, grad):
    quarter = d0.shape[0]
    for i, ref in enumerate((d0, d1, d2, d3)):
        grad[i * quarter : i * quarter + quarter, :] = ref[...]
    wide = place.shape[1]
    grad_t = dot(grad[...], one_hot(place), TN)
    product = grad_t * out_t[...].astype(f32)
    which = lax.broadcasted_iota(jnp.int32, (EXTRA, wide), 0)
    for head in range(2):
        delta = jnp.sum(product[head * HD : head * HD + HD], axis=0, keepdims=True)
        for side, ref in enumerate((ps, po)):

            @pl.when(head == (ctx[0] % 2 if side == 0 else 1 - ctx[0] % 2))
            def _():
                ref[:HD, :] = grad_t[head * HD : head * HD + HD].astype(bf16)
                rows = split3(delta) + split3(-logs[side, 0:1, :])
                tail = jnp.where(which == 6, 1.0, 0.0)
                for i, piece in enumerate(rows):
                    tail = jnp.where(which == i, piece, tail)
                ref[HD:, :] = tail.astype(bf16)


def backward_kernel(ctx, counts, *refs, blocks, starts, first, last):
    refs = list(refs)

    def take(count):
        taken = refs[:count]
        del refs[:count]
        return taken

    pieces = len(starts)
    q_refs = take(blocks)
    g_refs = take(blocks)
    kv_refs = take(pieces)
    if not first:
        (dq_in,) = take(1)
    dq_refs = take(blocks) if last else take(1)
    out_refs = take(pieces + 1) if last else take(pieces)
    kaug, vaug, k_t, q_all, g_all, dk, dv = take(7)
    if last:
        (dq_all,) = take(1)
    rows = kv_refs[0].shape[0]
    keys = pieces * rows
    wide = q_refs[0].shape[1]
    fill_keys(ctx, counts, starts, kv_refs, kaug)
    lane = lax.broadcasted_iota(jnp.int32, (rows, HD), 1)
    minus = jnp.where(lane < 3, -1.0, 0.0).astype(bf16)
    for part, ref in enumerate(kv_refs):
        where = slice(part * rows, part * rows + rows)
        vaug[where, :HD] = ref[:, HD:]
        vaug[where, HD:] = minus
        k_t[:, where] = ref[:, :HD].astype(f32).T.astype(bf16)
    dk[...] = jnp.zeros_like(dk)
    dv[...] = jnp.zeros_like(dv)
    blank = jnp.zeros((HD - EXTRA, wide), bf16)
    for i in range(blocks):
        q_all[i, :HD, :] = q_refs[i][...]
        q_all[i, HD : HD + EXTRA, :] = g_refs[i][HD:, :]
        q_all[i, HD + EXTRA :, :] = blank
        g_all[i, : HD + EXTRA, :] = g_refs[i][...]
        g_all[i, HD + EXTRA :, :] = blank

    def block(i, carry):
        query = q_all[i]
        grad = g_all[i]
        acc = jnp.zeros((HD, wide), f32) if first else dq_in[i]
        for j in range(keys // CHUNK):
            part = slice(j * CHUNK, j * CHUNK + CHUNK)
            p = jnp.exp2(dot(kaug[part, :], query, NN) * EXP2_SCALE)
            ds = (p * dot(vaug[part, :], grad, NN)).astype(bf16)
            dv[part, :] += dot(p.astype(bf16), grad[:HD], NT)
            dk[part, :] += dot(ds, query[:HD], NT)
            acc = acc + dot(k_t[:, part], ds, NN)
        if last:
            dq_all[i] = (acc * SCALE).astype(bf16)
        else:
            dq_refs[0][i] = acc
        return carry

    lax.fori_loop(0, blocks, block, 0)
    if last:
        for i in range(blocks):
            dq_refs[i][...] = dq_all[i]
    for part in range(pieces):
        where = slice(part * rows, part * rows + rows)
        if last and part == 0:
            out_refs[0][...] = dk[where, :] * SCALE
            out_refs[1][...] = dv[where, :]
        else:
            ref = out_refs[part + 1 if last else part]
            ref[:, :HD] = (dk[where, :] * SCALE).astype(bf16)
            ref[:, HD:] = dv[where, :].astype(bf16)


def backward(ctx, counts, q_blocks, g_blocks, kv_pieces, starts, before=None, last=False):
    blocks = len(q_blocks)
    pieces = len(kv_pieces)
    wide = q_blocks[0].shape[1]
    rows = kv_pieces[0].shape[0]
    keys = pieces * rows
    packed = ((rows, 2 * HD), bf16)
    if last:
        outs = [((HD, wide), bf16)] * blocks + [((rows, HD), f32)] * 2 + [packed] * (pieces - 1)
    else:
        outs = [((blocks, HD, wide), f32)] + [packed] * pieces
    scratch = [
        pltpu.VMEM((keys, 2 * HD), bf16),
        pltpu.VMEM((keys, 2 * HD), bf16),
        pltpu.VMEM((HD, keys), bf16),
        pltpu.VMEM((blocks, 2 * HD, wide), bf16),
        pltpu.VMEM((blocks, 2 * HD, wide), bf16),
        pltpu.VMEM((keys, HD), f32),
        pltpu.VMEM((keys, HD), f32),
    ]
    if last:
        scratch.append(pltpu.VMEM((blocks, HD, wide), bf16))
    args = [*q_blocks, *g_blocks, *kv_pieces] + ([] if before is None else [before])
    out = call(
        functools.partial(
            backward_kernel, blocks=blocks, starts=starts, first=before is None, last=last
        ),
        [SMEM] + [VMEM] * (len(args) + 1),
        outs,
        scratch,
        work=2 * 10**10,
    )(ctx, counts, *args)
    count = blocks if last else 1
    return (out[:blocks] if last else out[0]), out[count:]


def unrotate(x, c, s):
    return x * c - pltpu.roll(x, HD // 2, 1) * s


def query_grad_kernel(ctx, table, d0, d1, d2, d3, out):
    c, s = spread_angles(table)
    for which in range(2):

        @pl.when(ctx[0] % 2 == which)
        def _():
            for head, one, two in ((which, d0, d1), (1 - which, d2, d3)):
                total = one[...].astype(f32) + two[...].astype(f32)
                out[:, head * HD : head * HD + HD] = unrotate(total.T, c, s)


def key_grad_kernel(ctx, table, dk, dv, far, par, far_par, dk_out, dv_out):
    c, s = spread_angles(table)
    for which in range(2):

        @pl.when(ctx[0] % 2 == which)
        def _():
            cols = slice(which * HD, which * HD + HD)
            dk_out[:, cols] = unrotate(dk[...] + far[:, :HD].astype(f32), c, s)
            dv_out[:, cols] = dv[...] + far[:, HD:].astype(f32)
            cols = slice(HD - which * HD, 2 * HD - which * HD)
            total = par[...].astype(f32) + far_par[...].astype(f32)
            dk_out[:, cols] = unrotate(total[:, :HD], c, s)
            dv_out[:, cols] = total[:, HD:]


def ctx_swap(turn, flip):
    def target(x, z):
        x = (x, x ^ 1, 3 - x)[turn]
        return x * 2 + (z ^ flip)

    return [(x * 2 + z, target(x, z)) for x in range(4) for z in range(2)]


def send_ctx(array, turn, flip):
    return lax.ppermute(array, "ctx", ctx_swap(turn, flip))


def frame_xor(mask):
    return [(i, i ^ mask) for i in range(16)]


QUAD_MASKS = (0, 1, 8, 9)
Y_MASKS = (0, 2, 4, 6)


def send_frame(array, mask):
    return array if mask == 0 else lax.ppermute(array, "frame", frame_xor(mask))


def exchange(blocks):
    same, near, other, near_other = blocks
    return [same, send_ctx(near, 1, 0), send_ctx(other, 0, 1), send_ctx(near_other, 1, 1)]


def shards(
    queries,
    keys,
    values,
    query_frames,
    frame_counts,
    clip_of_frame,
    in_proj,
    mlp_up,
    mlp_down,
    reward_head,
):
    ctx_index = lax.axis_index("ctx")
    frame_index = lax.axis_index("frame")
    query_rows = queries.shape[0]
    key_rows = keys.shape[0]
    frame_slots = query_frames.shape[0]
    key_frames = frame_counts.shape[0]
    in_frame = jnp.arange(FTOK, dtype=jnp.int32)
    ctx = ctx_index.reshape(1).astype(jnp.int32)
    counts = frame_counts.reshape(-1, HD)
    packed_rows = ((key_rows, 2 * HD), bf16)
    key_table = (2, key_rows // FTOK + FTOK, HD)
    kv_own, kv_send, key_table = call(
        rotate_key_kernel,
        [SMEM] + [VMEM] * 2,
        [packed_rows] * 2 + [(key_table, f32)],
    )(ctx, keys, values)
    kv_far = send_ctx(kv_own, 2, 0)
    qs, qo, query_table = call(
        rotate_query_kernel,
        [SMEM] * 2 + [VMEM],
        [((HD, query_rows), bf16)] * 2 + [((2, frame_slots + FTOK, HD), f32)],
        [pltpu.VMEM((frame_slots, HD), f32)],
    )(ctx, query_frames, queries)
    q_blocks = exchange((qs, qs, qo, qo))
    kv_send, _ = lax.optimization_barrier((kv_send, qs))
    kv_par = send_ctx(kv_send, 0, 1)

    slot_index = jnp.arange(frame_slots, dtype=jnp.int32)
    same_clip = clip_of_frame[:, None] == clip_of_frame[None, :]
    earlier = slot_index[None, :] < slot_index[:, None]
    rank = jnp.sum(jnp.logical_and(same_clip, earlier), axis=1).astype(jnp.int32)
    away = clip_of_frame ^ frame_index
    quad = (away >> 3) * 2 + (away & 1)
    slot_place = (quad * 4 + ((away >> 1) & 3)) * CLIP + rank
    place = (slot_place[:, None] * FTOK + in_frame[None, :]).reshape(1, query_rows)
    frame_match = query_frames[:, None] == jnp.arange(key_frames, dtype=jnp.int32)[None, :]
    slot_counts = jnp.sum(jnp.where(frame_match, frame_counts[None, :], 0), axis=1)
    mine = slot_place[None, :] == jnp.arange(CLIP, dtype=jnp.int32)[:, None]
    my_counts = jnp.sum(jnp.where(mine, slot_counts[None, :], 0), axis=1).astype(jnp.int32)

    state = forward(ctx, counts, q_blocks, (kv_own, kv_far), (0, 2))
    kv_par, in_proj, _ = lax.optimization_barrier((kv_par, in_proj, state[1]))
    kv_far_par = send_ctx(kv_par, 2, 0)
    near = send_frame(in_proj, 8)
    state = forward(ctx, counts, q_blocks, (kv_par,), (1,), state)
    partial = forward(ctx, counts, q_blocks, (kv_far_par,), (3,), state, True)
    in_proj, near_late, _ = lax.optimization_barrier((in_proj, near, partial[0]))
    weights = (in_proj, send_frame(in_proj, 1), near_late, send_frame(near_late, 1))
    partial = exchange(partial)
    width = queries.shape[1]
    quarter = query_rows // 4
    out_t, logs, *chunks = call(
        combine_kernel,
        [SMEM] + [VMEM] * 5,
        [((width, query_rows), bf16), ((2, 8, query_rows), f32)] + [((quarter, width), bf16)] * 4,
        work=5 * 10**9,
    )(ctx, place, *partial)
    chunks = [send_frame(chunk, mask) for chunk, mask in zip(chunks, QUAD_MASKS)]
    vision = in_proj.shape[1]
    clip_rows = CLIP * FTOK
    inputs = call(
        project_kernel,
        [VMEM] * 8,
        [((clip_rows, vision), f32)] + [((clip_rows, vision), bf16)] * 3,
        work=5 * 10**9,
    )(*chunks, *weights)
    inputs = [send_frame(x, mask) for x, mask in zip(inputs, Y_MASKS)]
    input_grad, reward = reward_call(my_counts, inputs, reward_head, mlp_up, mlp_down)
    grads = [send_frame(input_grad, mask) for mask in Y_MASKS]
    grads = call(
        unproject_kernel,
        [VMEM] * 8,
        [((quarter, width), bf16)] * 4,
        [pltpu.VMEM((quarter, vision), bf16)],
    )(*grads, *weights)
    grads = [send_frame(grad, mask) for grad, mask in zip(grads, QUAD_MASKS)]
    packed = (HD + EXTRA, query_rows)
    gs, go = call(
        ungroup_kernel,
        [SMEM] + [VMEM] * 7,
        [(packed, bf16)] * 2,
        [pltpu.VMEM((query_rows, width), bf16)],
    )(ctx, place, *grads, out_t, logs)
    g_blocks = exchange((gs, gs, go, go))
    dq, (d_far_par,) = backward(ctx, counts, q_blocks, g_blocks, (kv_far_par,), (3,))
    d_far_par = send_ctx(d_far_par, 2, 1)
    dq, (d_par,) = backward(ctx, counts, q_blocks, g_blocks, (kv_par,), (1,), dq)
    d_par = send_ctx(d_par, 0, 1)
    dq, (d_far,) = backward(ctx, counts, q_blocks, g_blocks, (kv_far,), (2,), dq)
    d_far = send_ctx(d_far, 2, 0)
    dq, (dk_own, dv_own) = backward(
        ctx, counts, q_blocks, g_blocks, (kv_own,), (0,), dq, True
    )
    dq = exchange(dq)
    (query_grad,) = call(
        query_grad_kernel,
        [SMEM] + [VMEM] * 5,
        [((query_rows, width), f32)],
    )(ctx, query_table, *dq)
    key_grad, value_grad = call(
        key_grad_kernel,
        [SMEM] + [VMEM] * 6,
        [((key_rows, width), f32)] * 2,
    )(ctx, key_table, dk_own, dv_own, d_far, d_par, d_far_par)
    return query_grad, key_grad, value_grad, reward[0, :1]


def solution(mesh):
    return jax.shard_map(
        shards,
        mesh=mesh,
        in_specs=(
            P("ctx", "frame"),
            P("ctx", "frame"),
            P("ctx", "frame"),
            P("ctx"),
            P(),
            P("ctx"),
            P("frame", None),
            P(),
            P(),
            P(),
        ),
        out_specs=(P("ctx", "frame"), P("ctx", "frame"), P("ctx", "frame"), P(("ctx", "frame"))),
        check_vma=False,
    )
```

```python
import functools
import math

import jax
import jax.numpy as jnp
from jax import lax
from jax.experimental import pallas as pl
from jax.experimental.pallas import tpu as pltpu
from jax.sharding import PartitionSpec as P

HD = 128
FTOK = 16
CLIP = 2
EPSILON = 1e-05
SCALE = 1.0 / math.sqrt(HD)
EXP2_SCALE = SCALE * math.log2(math.e)
DEAD = -1e30
EXTRA = 16
CHUNK = 512


f32 = jnp.float32
bf16 = jnp.bfloat16

NN = (((1,), (0,)), ((), ()))
NT = (((1,), (1,)), ((), ()))
TN = (((0,), (0,)), ((), ()))

VMEM = pl.BlockSpec(memory_space=pltpu.VMEM)
SMEM = pl.BlockSpec(memory_space=pltpu.SMEM)


def dot(left, right, dims):
    return lax.dot_general(left, right, dims, preferred_element_type=f32)


def call(kernel, in_specs, outs, scratch=(), work=0, limit=8):
    return pl.pallas_call(
        kernel,
        cost_estimate=pl.CostEstimate(flops=work, transcendentals=0, bytes_accessed=1 << 20),
        out_shape=[jax.ShapeDtypeStruct(shape, dtype) for shape, dtype in outs],
        in_specs=in_specs,
        out_specs=[VMEM] * len(outs),
        scratch_shapes=list(scratch),
        compiler_params=pltpu.CompilerParams(vmem_limit_bytes=limit * 1024 * 1024),
    )


def split3(x):
    high = x.astype(bf16).astype(f32)
    rest = x - high
    middle = rest.astype(bf16).astype(f32)
    low = (rest - middle).astype(bf16).astype(f32)
    return high, middle, low


def angles(frame):
    lane = lax.broadcasted_iota(jnp.int32, (1, HD), 1).astype(f32)
    half_width = HD // 2
    lane = jnp.where(lane < half_width, lane, lane - half_width)
    angle = frame * jnp.exp(lane * (-math.log(10000.0) / half_width))
    return jnp.cos(angle), jnp.sin(angle)


def spread_angles(table):
    slots = table.shape[1] - FTOK
    cf, sf = table[0, :slots, :], table[1, :slots, :]
    ct, st = table[0, slots:, :], table[1, slots:, :]
    c = cf[:, None, :] * ct[None] - sf[:, None, :] * st[None]
    s = sf[:, None, :] * ct[None] + cf[:, None, :] * st[None]
    rows = slots * FTOK
    lane = lax.broadcasted_iota(jnp.int32, (rows, HD), 1)
    return c.reshape(rows, HD), jnp.where(lane < HD // 2, -1.0, 1.0) * s.reshape(rows, HD)


def fill_table(table, frames):
    slots = table.shape[1] - FTOK
    table[0, :slots, :], table[1, :slots, :] = angles(frames * FTOK)
    token = lax.broadcasted_iota(jnp.int32, (FTOK, HD), 0).astype(f32)
    table[0, slots:, :], table[1, slots:, :] = angles(token)


def rotate_kernel(ctx, frames_any, q_any, k_any, v_any, *refs):
    kv_own, kv_send, kv_high, key_table, q_own, q_send, query_table = refs[:7]
    q, k, v, frames, places, sems = refs[7:]
    pairs = ((k_any, k), (v_any, v), (q_any, q), (frames_any, frames))
    copies = [pltpu.make_async_copy(one, two, sems.at[i]) for i, (one, two) in enumerate(pairs)]
    for copy in copies:
        copy.start()
    slots = k.shape[0] // FTOK
    row = lax.broadcasted_iota(jnp.int32, (slots, HD), 0)
    fill_table(key_table, (row + ctx[0] * slots).astype(f32))
    c, s = spread_angles(key_table)
    for copy in copies:
        copy.wait()
    high = kv_high.shape[0]
    for which in range(2):

        @pl.when(ctx[0] % 2 == which)
        def _():
            for side, out in ((which, kv_own), (1 - which, kv_send)):
                cols = slice(side * HD, side * HD + HD)
                head = k[:, cols].astype(f32)
                turned = head * c + pltpu.roll(head, HD // 2, 1) * s
                out[:, :HD] = turned.astype(bf16)
                out[:, HD:] = v[:, cols]

    kv_high[...] = kv_send[-high:, :]
    for i in range(places.shape[0]):
        places[i : i + 1, :] = jnp.full((1, HD), frames[i].astype(f32))
    fill_table(query_table, places[...])
    c, s = spread_angles(query_table)
    for which in range(2):

        @pl.when(ctx[0] % 2 == which)
        def _():
            for side, out in ((which, q_own), (1 - which, q_send)):
                head = q[:, side * HD : side * HD + HD].astype(f32)
                turned = head * c + pltpu.roll(head, HD // 2, 1) * s
                out[...] = turned.T.astype(bf16)


def plan_kernel(frame, clips, frames, counts, place, live, seen):
    slots = clips.shape[0]
    for i in range(seen.shape[0]):
        seen[i] = 0
    lane = lax.broadcasted_iota(jnp.int32, place.shape, 1)
    slot = lane // FTOK
    total = jnp.zeros(place.shape, jnp.int32)
    for i in range(slots):
        clip = clips[i]
        rank = seen[clip]
        seen[clip] = rank + 1
        away = clip ^ frame[0]
        spot = (((away // 8) * 2 + away % 2) * 4 + (away // 2) % 4) * CLIP + rank
        total = jnp.where(slot == i, spot * FTOK, total)

        @pl.when(away == 0)
        def _():
            live[rank] = counts[frames[i]]

    place[...] = total + lane % FTOK


def fill_keys(ctx, counts, starts, kv_refs, kaug):
    rows = kv_refs[0].shape[0]
    lane = lax.broadcasted_iota(jnp.int32, (rows, HD), 1)
    row = lax.broadcasted_iota(jnp.int32, (rows, HD), 0)
    ones = jnp.where((lane >= 3) & (lane < 6), 1.0, 0.0)
    live = jnp.sum(jnp.sum(counts[...].astype(f32), axis=0, keepdims=True), axis=1, keepdims=True)
    me = ctx[0]
    owners = (me, me ^ 1, 6 - me + 2 * (me % 2), 7 - me)
    for part, ref in enumerate(kv_refs):
        owner, index, parts = starts[part]
        place = (row + (owners[owner] * parts + index) * rows).astype(f32)
        bias = jnp.where(place < live, 0.0, DEAD)
        kaug[part * rows : part * rows + rows, :HD] = ref[:, :HD]
        kaug[part * rows : part * rows + rows, HD:] = jnp.where(lane == 6, bias, ones).astype(bf16)


def forward_kernel(ctx, counts, *refs, blocks, starts, first, last):
    refs = list(refs)

    def take(count):
        taken = refs[:count]
        del refs[:count]
        return taken

    pieces = len(starts)
    if first:
        q_refs = take(blocks)
    else:
        (q_all,) = take(1)
    kv_refs = take(pieces)
    if not first:
        acc_in, stat_in = take(2)
    if last:
        out_refs = take(blocks)
    else:
        acc_out, stat_out = take(2)
    if first:
        (q_all,) = take(1)
    kaug, v_t, *scores = take(4)
    if last:
        (out_all,) = take(1)
    rows = kv_refs[0].shape[0]
    keys = pieces * rows
    wide = q_all.shape[2]
    fill_keys(ctx, counts, starts, kv_refs, kaug)
    for part, ref in enumerate(kv_refs):
        v_t[:, part * rows : part * rows + rows] = ref[:, HD:].astype(f32).T.astype(bf16)
    if first:
        sub = lax.broadcasted_iota(jnp.int32, (HD, wide), 0)
        tail = jnp.where(sub == 6, 1.0, 0.0).astype(bf16)
        for i in range(blocks):
            q_all[i, :HD, :] = q_refs[i][...]
            q_all[i, HD:, :] = tail
    spans = [slice(j * CHUNK, j * CHUNK + CHUNK) for j in range(keys // CHUNK)]

    def score(i, slot, span, top):
        s = dot(kaug[span, :], q_all[i], NN)
        scores[slot][span, :] = s
        return jnp.maximum(top, jnp.max(s, axis=0, keepdims=True))

    def start(i):
        return jnp.full((1, wide), -jnp.inf, f32) if first else stat_in[i, 0:1, :]

    def block(i, slot, top, follow):
        if first:
            total = jnp.zeros((1, wide), f32)
            acc = jnp.zeros((HD, wide), f32)
        else:
            shrink = jnp.exp2((stat_in[i, 0:1, :] - top) * EXP2_SCALE)
            total = stat_in[i, 1:2, :] * shrink
            acc = acc_in[i] * shrink
        following = start(follow)
        for span in spans:
            following = score(follow, 1 - slot, span, following)
            p = jnp.exp2((scores[slot][span, :] - top) * EXP2_SCALE)
            total = total + jnp.sum(p, axis=0, keepdims=True)
            acc = acc + dot(v_t[:, span], p.astype(bf16), NN)
        if not last:
            acc_out[i] = acc
            which = lax.broadcasted_iota(jnp.int32, (8, wide), 0)
            stat_out[i] = jnp.where(which == 0, top, total)
        else:
            out_all[i, :HD, :] = (acc / total).astype(bf16)
            high, middle, low = split3(top + jnp.log(total) * (1.0 / SCALE))
            which = lax.broadcasted_iota(jnp.int32, (EXTRA, wide), 0)
            rest = jnp.where(which == 1, middle, jnp.where(which == 2, low, 0.0))
            out_all[i, HD:, :] = jnp.where(which == 0, high, rest).astype(bf16)
        return following

    top = start(0)
    for span in spans:
        top = score(0, 0, span, top)

    def pair(t, top):
        middle = block(2 * t, 0, top, 2 * t + 1)
        return block(2 * t + 1, 1, middle, jnp.minimum(2 * t + 2, blocks - 1))

    lax.fori_loop(0, blocks // 2, pair, top)
    if last:
        for i in range(blocks):
            out_refs[i][...] = out_all[i]


def forward(ctx, counts, q_blocks, kv_pieces, starts, before=(), last=False):
    first = not before
    blocks, wide = (len(q_blocks), q_blocks[0].shape[1]) if first else q_blocks.shape[::2]
    keys = len(kv_pieces) * kv_pieces[0].shape[0]
    if last:
        outs = [((HD + EXTRA, wide), bf16)] * blocks
    else:
        outs = [((blocks, HD, wide), f32), ((blocks, 8, wide), f32)]
    if first:
        outs.append(((blocks, 2 * HD, wide), bf16))
    args = [*(q_blocks if first else [q_blocks]), *kv_pieces, *before]
    return call(
        functools.partial(forward_kernel, blocks=blocks, starts=starts, first=first, last=last),
        [SMEM] + [VMEM] * (len(args) + 1),
        outs,
        [
            pltpu.VMEM((keys, 2 * HD), bf16),
            pltpu.VMEM((HD, keys), bf16),
            pltpu.VMEM((keys, wide), f32),
            pltpu.VMEM((keys, wide), f32),
        ]
        + ([pltpu.VMEM((blocks, HD + EXTRA, wide), bf16)] if last else []),
        work=10**10,
        limit=13 if first else 8,
    )(ctx, counts, *args)


def one_hot(place):
    rows = place.shape[1]
    row = lax.broadcasted_iota(jnp.int32, (rows, rows), 0)
    return jnp.where(row == place[...], 1.0, 0.0).astype(bf16)


def combine_kernel(ctx, place, *refs):
    partial, (out_t, logs, c0, c1, c2, c3) = refs[:4], refs[4:]
    wide = partial[0].shape[1]
    for side in range(2):
        sums = []
        for ref in partial[2 * side : 2 * side + 2]:
            tail = ref[HD:, :].astype(f32)
            sums.append(tail[0:1] + tail[1:2] + tail[2:3])
        top = functools.reduce(jnp.maximum, sums)
        weight = [jnp.exp2((s - top) * EXP2_SCALE) for s in sums]
        total = sum(weight)
        acc = jnp.zeros((HD, wide), f32)
        for w, ref in zip(weight, partial[2 * side : 2 * side + 2]):
            acc = acc + (w / total) * ref[:HD, :].astype(f32)
        logs[side, :, :] = jnp.broadcast_to(top + jnp.log(total) * (1.0 / SCALE), (8, wide))
        head = ctx[0] % 2 if side == 0 else 1 - ctx[0] % 2
        out_t[pl.ds(pl.multiple_of(head * HD, HD), HD), :] = acc.astype(bf16)
    grouped = dot(one_hot(place), out_t[...], NT).astype(bf16)
    quarter = wide // 4
    for i, ref in enumerate((c0, c1, c2, c3)):
        ref[...] = grouped[i * quarter : i * quarter + quarter]


def project_kernel(o0, o1, o2, o3, w0, w1, w2, w3, x0, x1, x2, x3):
    total = None
    for o, w in ((o0, w0), (o1, w1), (o2, w2), (o3, w3)):
        term = dot(o[...], w[...], NN)
        total = term if total is None else total + term
    rows = x0.shape[0]
    for i, ref in enumerate((x0, x1, x2, x3)):
        ref[...] = total[i * rows : i * rows + rows].astype(ref.dtype)


def unproject_kernel(g0, g1, g2, g3, w0, w1, w2, w3, d0, d1, d2, d3, g):
    rows = g0.shape[0]
    for i, ref in enumerate((g0, g1, g2, g3)):
        g[i * rows : i * rows + rows, :] = ref[...]
    for w, d in ((w0, d0), (w1, d1), (w2, d2), (w3, d3)):
        d[...] = dot(g[...], w[...], NT).astype(bf16)


def center(x):
    mean = jnp.mean(x, axis=1, keepdims=True)
    shifted = x - mean
    rate = lax.rsqrt(jnp.mean(shifted * shifted, axis=1, keepdims=True) + EPSILON)
    return shifted * rate, rate


def center_grad(grad, normed, rate):
    return rate * (
        grad
        - jnp.mean(grad, axis=1, keepdims=True)
        - normed * jnp.mean(grad * normed, axis=1, keepdims=True)
    )


def reward_kernel(counts, x0, x1, x2, x3, head, up, down, grad_out, reward_out, slopes):
    steps, _, part = slopes.shape
    vision = up.shape[0]

    def piece(j):
        return pl.ds(pl.multiple_of(j * part, part), part)

    rows = x0.shape[0]

    def live(shape, axis):
        row = lax.broadcasted_iota(jnp.int32, shape, axis)
        left = jnp.where(row < FTOK, counts[0], counts[1] + FTOK)
        return jnp.where(row < left, 1.0, 0.0)

    x = x0[...].astype(f32) + x1[...].astype(f32) + x2[...].astype(f32) + x3[...].astype(f32)
    normed, rate = center(x)
    low_normed = normed.astype(bf16)
    c0 = math.sqrt(2.0 / math.pi)
    c1 = 0.044715

    def upward(j, hidden):
        before = dot(low_normed, up[:, piece(j)], NN)
        square = before * before
        tanh = jnp.tanh(c0 * before * (1.0 + c1 * square))
        half = 0.5 * (1.0 + tanh)
        slope = half + 0.5 * before * (1.0 - tanh * tanh) * (c0 * (1.0 + 3.0 * c1 * square))
        slopes[j] = slope
        return hidden + dot((before * half).astype(bf16), down[piece(j), :], NN)

    hidden = lax.fori_loop(0, steps, upward, jnp.zeros((rows, vision), f32))
    alive = live((rows, 1), 0)
    count = jnp.sum(alive, axis=0, keepdims=True)
    pooled = jnp.sum(hidden * alive, axis=0, keepdims=True) / count
    pooled_normed, pooled_rate = center(pooled)
    reward = count * jnp.sum(pooled_normed * head[...], axis=1, keepdims=True)
    reward_out[...] = jnp.broadcast_to(reward, reward_out.shape)
    pooled_grad = center_grad(count * head[...], pooled_normed, pooled_rate) / count
    high, middle, low = split3(pooled_grad)
    which = lax.broadcasted_iota(jnp.int32, (EXTRA, vision), 0)
    pieces = jnp.where(which == 0, high, jnp.where(which == 1, middle, jnp.where(which == 2, low, 0.0)))
    pieces_b = pieces.astype(bf16)
    alive_t = live((1, rows), 1)

    def downward(j, normed_grad):
        spread = jnp.sum(dot(pieces_b, down[piece(j), :], NT), axis=0, keepdims=True)
        before_grad = (spread * slopes[j] * alive).astype(bf16)
        return normed_grad + dot(before_grad, up[:, piece(j)], NT)

    normed_grad = lax.fori_loop(0, steps, downward, jnp.zeros((rows, vision), f32))
    grad_out[...] = center_grad(normed_grad, normed, rate).astype(bf16)


def reward_call(counts, inputs, head, mlp_up, mlp_down):
    vision, hidden = mlp_up.shape
    steps = 8
    part = hidden // steps
    rows = inputs[0].shape[0]
    return call(
        reward_kernel,
        [SMEM] + [VMEM] * 7,
        [((rows, vision), bf16), ((8, HD), f32)],
        [
            pltpu.VMEM((steps, rows, part), f32),
        ],
    )(counts, *inputs, head.reshape(1, -1), mlp_up, mlp_down)


def ungroup_kernel(ctx, place, d0, d1, d2, d3, out_t, logs, ps, po, grad):
    quarter = d0.shape[0]
    for i, ref in enumerate((d0, d1, d2, d3)):
        grad[i * quarter : i * quarter + quarter, :] = ref[...]
    wide = place.shape[1]
    grad_t = dot(grad[...], one_hot(place), TN)
    product = grad_t * out_t[...].astype(f32)
    which = lax.broadcasted_iota(jnp.int32, (EXTRA, wide), 0)
    for head in range(2):
        delta = jnp.sum(product[head * HD : head * HD + HD], axis=0, keepdims=True)
        for side, ref in enumerate((ps, po)):

            @pl.when(head == (ctx[0] % 2 if side == 0 else 1 - ctx[0] % 2))
            def _():
                ref[:HD, :] = grad_t[head * HD : head * HD + HD].astype(bf16)
                rows = split3(delta) + split3(-logs[side, 0:1, :])
                tail = jnp.where(which == 6, 1.0, 0.0)
                for i, piece in enumerate(rows):
                    tail = jnp.where(which == i, piece, tail)
                ref[HD:, :] = tail.astype(bf16)


def backward_kernel(ctx, counts, *refs, blocks, starts, first, last):
    refs = list(refs)

    def take(count):
        taken = refs[:count]
        del refs[:count]
        return taken

    pieces = len(starts)
    (q_in,) = take(1)
    g_refs = take(blocks)
    kv_refs = take(pieces)
    if not first:
        (dq_in,) = take(1)
    dq_refs = take(blocks) if last else take(1)
    out_refs = take(2) if last else take(1)
    kaug, vaug, k_t, q_all, g_all, dk, dv = take(7)
    if last:
        (dq_all,) = take(1)
    rows = kv_refs[0].shape[0]
    keys = pieces * rows
    wide = q_in.shape[2]
    fill_keys(ctx, counts, starts, kv_refs, kaug)
    lane = lax.broadcasted_iota(jnp.int32, (rows, HD), 1)
    minus = jnp.where(lane < 3, -1.0, 0.0).astype(bf16)
    for part, ref in enumerate(kv_refs):
        where = slice(part * rows, part * rows + rows)
        vaug[where, :HD] = ref[:, HD:]
        vaug[where, HD:] = minus
        k_t[:, where] = ref[:, :HD].astype(f32).T.astype(bf16)
    dk[...] = jnp.zeros_like(dk)
    dv[...] = jnp.zeros_like(dv)
    blank = jnp.zeros((HD - EXTRA, wide), bf16)
    for i in range(blocks):
        q_all[i, :HD, :] = q_in[i, :HD, :]
        q_all[i, HD : HD + EXTRA, :] = g_refs[i][HD:, :]
        q_all[i, HD + EXTRA :, :] = blank
        g_all[i, : HD + EXTRA, :] = g_refs[i][...]
        g_all[i, HD + EXTRA :, :] = blank

    def block(i, carry):
        query = q_all[i]
        grad = g_all[i]
        acc = jnp.zeros((HD, wide), f32) if first else dq_in[i]
        for j in range(keys // CHUNK):
            part = slice(j * CHUNK, j * CHUNK + CHUNK)
            p = jnp.exp2(dot(kaug[part, :], query, NN) * EXP2_SCALE)
            ds = (p * dot(vaug[part, :], grad, NN)).astype(bf16)
            dv[part, :] += dot(p.astype(bf16), grad[:HD], NT)
            dk[part, :] += dot(ds, query[:HD], NT)
            acc = acc + dot(k_t[:, part], ds, NN)
        if last:
            dq_all[i] = (acc * SCALE).astype(bf16)
        else:
            dq_refs[0][i] = acc
        return carry

    lax.fori_loop(0, blocks, block, 0)
    if last:
        for i in range(blocks):
            dq_refs[i][...] = dq_all[i]
    if last:
        out_refs[0][...] = dk[...] * SCALE
        out_refs[1][...] = dv[...]
    else:
        out_refs[0][:, :HD] = (dk[...] * SCALE).astype(bf16)
        out_refs[0][:, HD:] = dv[...].astype(bf16)


def backward(ctx, counts, q_blocks, g_blocks, kv_pieces, starts, before=None, last=False):
    blocks, _, wide = q_blocks.shape
    pieces = len(kv_pieces)
    rows = kv_pieces[0].shape[0]
    keys = pieces * rows
    if last:
        outs = [((HD, wide), bf16)] * blocks + [((keys, HD), f32)] * 2
    else:
        outs = [((blocks, HD, wide), f32), ((keys, 2 * HD), bf16)]
    scratch = [
        pltpu.VMEM((keys, 2 * HD), bf16),
        pltpu.VMEM((keys, 2 * HD), bf16),
        pltpu.VMEM((HD, keys), bf16),
        pltpu.VMEM((blocks, 2 * HD, wide), bf16),
        pltpu.VMEM((blocks, 2 * HD, wide), bf16),
        pltpu.VMEM((keys, HD), f32),
        pltpu.VMEM((keys, HD), f32),
    ]
    if last:
        scratch.append(pltpu.VMEM((blocks, HD, wide), bf16))
    args = [q_blocks, *g_blocks, *kv_pieces] + ([] if before is None else [before])
    out = call(
        functools.partial(
            backward_kernel, blocks=blocks, starts=starts, first=before is None, last=last
        ),
        [SMEM] + [VMEM] * (len(args) + 1),
        outs,
        scratch,
        work=2 * 10**10,
    )(ctx, counts, *args)
    count = blocks if last else 1
    return (out[:blocks] if last else out[0]), out[count:]


def unrotate(x, c, s):
    return x * c - pltpu.roll(x, HD // 2, 1) * s


def query_grad_kernel(ctx, table, d0, d1, d2, d3, out):
    c, s = spread_angles(table)
    for which in range(2):

        @pl.when(ctx[0] % 2 == which)
        def _():
            for head, one, two in ((which, d0, d1), (1 - which, d2, d3)):
                total = one[...].astype(f32) + two[...].astype(f32)
                out[:, head * HD : head * HD + HD] = unrotate(total.T, c, s)


def key_grad_kernel(ctx, table, dk, dv, far, par, far_par, dk_out, dv_out):
    c, s = spread_angles(table)
    for which in range(2):

        @pl.when(ctx[0] % 2 == which)
        def _():
            cols = slice(which * HD, which * HD + HD)
            dk_out[:, cols] = unrotate(dk[...] + far[:, :HD].astype(f32), c, s)
            dv_out[:, cols] = dv[...] + far[:, HD:].astype(f32)
            cols = slice(HD - which * HD, 2 * HD - which * HD)
            total = par[...].astype(f32) + far_par[...].astype(f32)
            dk_out[:, cols] = unrotate(total[:, :HD], c, s)
            dv_out[:, cols] = total[:, HD:]


def ctx_swap(turn, flip):
    def target(x, z):
        x = (x, x ^ 1, 3 - x)[turn]
        return x * 2 + (z ^ flip)

    return [(x * 2 + z, target(x, z)) for x in range(4) for z in range(2)]


def send_ctx(array, turn, flip):
    return lax.ppermute(array, "ctx", ctx_swap(turn, flip))


def frame_xor(mask):
    return [(i, i ^ mask) for i in range(16)]


QUAD_MASKS = (0, 1, 8, 9)
Y_MASKS = (0, 2, 4, 6)


def send_frame(array, mask):
    return array if mask == 0 else lax.ppermute(array, "frame", frame_xor(mask))


def exchange(blocks):
    same, near, other, near_other = blocks
    return [same, send_ctx(near, 1, 0), send_ctx(other, 0, 1), send_ctx(near_other, 1, 1)]


def shards(
    queries,
    keys,
    values,
    query_frames,
    frame_counts,
    clip_of_frame,
    in_proj,
    mlp_up,
    mlp_down,
    reward_head,
):
    ctx_index = lax.axis_index("ctx")
    frame_index = lax.axis_index("frame")
    query_rows = queries.shape[0]
    key_rows = keys.shape[0]
    frame_slots = query_frames.shape[0]
    ctx = ctx_index.reshape(1).astype(jnp.int32)
    counts = frame_counts.reshape(-1, HD)
    packed_rows = ((key_rows, 2 * HD), bf16)
    any_space = pl.BlockSpec(memory_space=pltpu.HBM)
    high_rows = key_rows // 2
    kv_own, kv_send, kv_high, key_table, qs, qo, query_table = call(
        rotate_kernel,
        [SMEM] + [any_space] * 4,
        [packed_rows] * 2
        + [((high_rows, 2 * HD), bf16), ((2, key_rows // FTOK + FTOK, HD), f32)]
        + [((HD, query_rows), bf16)] * 2
        + [((2, frame_slots + FTOK, HD), f32)],
        [
            pltpu.VMEM(queries.shape, bf16),
            pltpu.VMEM(keys.shape, bf16),
            pltpu.VMEM(values.shape, bf16),
            pltpu.SMEM((frame_slots,), jnp.int32),
            pltpu.VMEM((frame_slots, HD), f32),
            pltpu.SemaphoreType.DMA((4,)),
        ],
    )(ctx, query_frames, queries, keys, values)
    kv_far = send_ctx(kv_own, 2, 0)
    q_blocks = exchange((qs, qs, qo, qo))
    kv_par = send_ctx(kv_send, 0, 1)

    place, my_counts = pl.pallas_call(
        plan_kernel,
        out_shape=[
            jax.ShapeDtypeStruct((1, query_rows), jnp.int32),
            jax.ShapeDtypeStruct((CLIP,), jnp.int32),
        ],
        in_specs=[SMEM] * 4,
        out_specs=[VMEM, SMEM],
        scratch_shapes=[pltpu.SMEM((frame_slots // CLIP,), jnp.int32)],
        compiler_params=pltpu.CompilerParams(vmem_limit_bytes=8 * 1024 * 1024),
    )(frame_index.reshape(1).astype(jnp.int32), clip_of_frame, query_frames, frame_counts)

    *state, q_blocks = forward(
        ctx, counts, q_blocks, (kv_own, kv_far), ((0, 0, 1), (2, 0, 1))
    )
    kv_high, _ = lax.optimization_barrier((kv_high, state[1]))
    kv_par, _ = lax.optimization_barrier((kv_par, state[1]))
    kv_far_high = send_ctx(kv_high, 2, 1)
    kv_far_low = send_ctx(kv_par[:high_rows], 2, 0)
    state = forward(ctx, counts, q_blocks, (kv_par,), ((1, 0, 1),), state)
    in_proj, _ = lax.optimization_barrier((in_proj, state[1]))
    near = send_frame(in_proj, 8)
    kv_far_par = (kv_far_low, kv_far_high)
    far_par = ((3, 0, 2), (3, 1, 2))
    partial = forward(ctx, counts, q_blocks, kv_far_par, far_par, state, True)
    in_proj, near_late, _ = lax.optimization_barrier((in_proj, near, partial[0]))
    weights = (in_proj, send_frame(in_proj, 1), near_late, send_frame(near_late, 1))
    partial = exchange(partial)
    width = queries.shape[1]
    quarter = query_rows // 4
    out_t, logs, *chunks = call(
        combine_kernel,
        [SMEM] + [VMEM] * 5,
        [((width, query_rows), bf16), ((2, 8, query_rows), f32)] + [((quarter, width), bf16)] * 4,
        work=5 * 10**9,
    )(ctx, place, *partial)
    chunks = [send_frame(chunk, mask) for chunk, mask in zip(chunks, QUAD_MASKS)]
    vision = in_proj.shape[1]
    clip_rows = CLIP * FTOK
    inputs = call(
        project_kernel,
        [VMEM] * 8,
        [((clip_rows, vision), f32)] + [((clip_rows, vision), bf16)] * 3,
        work=5 * 10**9,
    )(*chunks, *weights)
    inputs = [send_frame(x, mask) for x, mask in zip(inputs, Y_MASKS)]
    input_grad, reward = reward_call(my_counts, inputs, reward_head, mlp_up, mlp_down)
    grads = [send_frame(input_grad, mask) for mask in Y_MASKS]
    grads = call(
        unproject_kernel,
        [VMEM] * 8,
        [((quarter, width), bf16)] * 4,
        [pltpu.VMEM((quarter, vision), bf16)],
    )(*grads, *weights)
    grads = [send_frame(grad, mask) for grad, mask in zip(grads, QUAD_MASKS)]
    packed = (HD + EXTRA, query_rows)
    gs, go = call(
        ungroup_kernel,
        [SMEM] + [VMEM] * 7,
        [(packed, bf16)] * 2,
        [pltpu.VMEM((query_rows, width), bf16)],
    )(ctx, place, *grads, out_t, logs)
    g_blocks = exchange((gs, gs, go, go))
    dq, (d_far_par,) = backward(ctx, counts, q_blocks, g_blocks, kv_far_par, far_par)
    d_far_par = send_ctx(d_far_par, 2, 1)
    dq, (d_par,) = backward(ctx, counts, q_blocks, g_blocks, (kv_par,), ((1, 0, 1),), dq)
    d_par = send_ctx(d_par, 0, 1)
    dq, (d_far,) = backward(ctx, counts, q_blocks, g_blocks, (kv_far,), ((2, 0, 1),), dq)
    d_far = send_ctx(d_far, 2, 0)
    dq, (dk_own, dv_own) = backward(
        ctx, counts, q_blocks, g_blocks, (kv_own,), ((0, 0, 1),), dq, True
    )
    dq = exchange(dq)
    (query_grad,) = call(
        query_grad_kernel,
        [SMEM] + [VMEM] * 5,
        [((query_rows, width), f32)],
    )(ctx, query_table, *dq)
    key_grad, value_grad = call(
        key_grad_kernel,
        [SMEM] + [VMEM] * 6,
        [((key_rows, width), f32)] * 2,
    )(ctx, key_table, dk_own, dv_own, d_far, d_par, d_far_par)
    return query_grad, key_grad, value_grad, reward[0, :1]


def solution(mesh):
    return jax.shard_map(
        shards,
        mesh=mesh,
        in_specs=(
            P("ctx", "frame"),
            P("ctx", "frame"),
            P("ctx", "frame"),
            P("ctx"),
            P(),
            P("ctx"),
            P("frame", None),
            P(),
            P(),
            P(),
        ),
        out_specs=(P("ctx", "frame"), P("ctx", "frame"), P("ctx", "frame"), P(("ctx", "frame"))),
        check_vma=False,
    )
```

```python
import functools
import math

import jax
import jax.numpy as jnp
from jax import lax
from jax.experimental import pallas as pl
from jax.experimental.pallas import tpu as pltpu
from jax.sharding import PartitionSpec as P

HD = 128
FTOK = 16
CLIP = 2
EPSILON = 1e-05
SCALE = 1.0 / math.sqrt(HD)
EXP2_SCALE = SCALE * math.log2(math.e)
DEAD = -1e30
EXTRA = 16
CHUNK = 512


f32 = jnp.float32
bf16 = jnp.bfloat16

NN = (((1,), (0,)), ((), ()))
NT = (((1,), (1,)), ((), ()))
TN = (((0,), (0,)), ((), ()))

VMEM = pl.BlockSpec(memory_space=pltpu.VMEM)
SMEM = pl.BlockSpec(memory_space=pltpu.SMEM)


def dot(left, right, dims):
    return lax.dot_general(left, right, dims, preferred_element_type=f32)


def call(kernel, in_specs, outs, scratch=(), work=0, limit=8):
    return pl.pallas_call(
        kernel,
        cost_estimate=pl.CostEstimate(flops=work, transcendentals=0, bytes_accessed=1 << 20),
        out_shape=[jax.ShapeDtypeStruct(shape, dtype) for shape, dtype in outs],
        in_specs=in_specs,
        out_specs=[VMEM] * len(outs),
        scratch_shapes=list(scratch),
        compiler_params=pltpu.CompilerParams(vmem_limit_bytes=limit * 1024 * 1024),
    )


def split3(x):
    high = x.astype(bf16).astype(f32)
    rest = x - high
    middle = rest.astype(bf16).astype(f32)
    low = (rest - middle).astype(bf16).astype(f32)
    return high, middle, low


def angles(frame):
    lane = lax.broadcasted_iota(jnp.int32, (1, HD), 1).astype(f32)
    half_width = HD // 2
    lane = jnp.where(lane < half_width, lane, lane - half_width)
    angle = frame * jnp.exp(lane * (-math.log(10000.0) / half_width))
    return jnp.cos(angle), jnp.sin(angle)


def spread_angles(table):
    slots = table.shape[1] - FTOK
    cf, sf = table[0, :slots, :], table[1, :slots, :]
    ct, st = table[0, slots:, :], table[1, slots:, :]
    c = cf[:, None, :] * ct[None] - sf[:, None, :] * st[None]
    s = sf[:, None, :] * ct[None] + cf[:, None, :] * st[None]
    rows = slots * FTOK
    lane = lax.broadcasted_iota(jnp.int32, (rows, HD), 1)
    return c.reshape(rows, HD), jnp.where(lane < HD // 2, -1.0, 1.0) * s.reshape(rows, HD)


def fill_table(table, frames):
    slots = table.shape[1] - FTOK
    table[0, :slots, :], table[1, :slots, :] = angles(frames * FTOK)
    token = lax.broadcasted_iota(jnp.int32, (FTOK, HD), 0).astype(f32)
    table[0, slots:, :], table[1, slots:, :] = angles(token)


def rotate_kernel(ctx, frames_any, q_any, k_any, v_any, *refs):
    kv_own, kv_send, kv_high, key_table, q_own, q_send, query_table = refs[:7]
    q, k, v, frames, places, sems = refs[7:]
    pairs = ((k_any, k), (v_any, v), (q_any, q), (frames_any, frames))
    copies = [pltpu.make_async_copy(one, two, sems.at[i]) for i, (one, two) in enumerate(pairs)]
    for copy in copies:
        copy.start()
    slots = k.shape[0] // FTOK
    row = lax.broadcasted_iota(jnp.int32, (slots, HD), 0)
    fill_table(key_table, (row + ctx[0] * slots).astype(f32))
    c, s = spread_angles(key_table)
    for copy in copies:
        copy.wait()
    high = kv_high.shape[0]
    for which in range(2):

        @pl.when(ctx[0] % 2 == which)
        def _():
            for side, out in ((which, kv_own), (1 - which, kv_send)):
                cols = slice(side * HD, side * HD + HD)
                head = k[:, cols].astype(f32)
                turned = head * c + pltpu.roll(head, HD // 2, 1) * s
                out[:, :HD] = turned.astype(bf16)
                out[:, HD:] = v[:, cols]

    kv_high[...] = kv_send[-high:, :]
    for i in range(places.shape[0]):
        places[i : i + 1, :] = jnp.full((1, HD), frames[i].astype(f32))
    fill_table(query_table, places[...])
    c, s = spread_angles(query_table)
    for which in range(2):

        @pl.when(ctx[0] % 2 == which)
        def _():
            for side, out in ((which, q_own), (1 - which, q_send)):
                head = q[:, side * HD : side * HD + HD].astype(f32)
                turned = head * c + pltpu.roll(head, HD // 2, 1) * s
                out[...] = turned.T.astype(bf16)


def fill_keys(ctx, counts, starts, kv_refs, kaug):
    rows = kv_refs[0].shape[0]
    lane = lax.broadcasted_iota(jnp.int32, (rows, HD), 1)
    row = lax.broadcasted_iota(jnp.int32, (rows, HD), 0)
    ones = jnp.where((lane >= 3) & (lane < 6), 1.0, 0.0)
    live = jnp.sum(jnp.sum(counts[...].astype(f32), axis=0, keepdims=True), axis=1, keepdims=True)
    me = ctx[0]
    owners = (me, me ^ 1, 6 - me + 2 * (me % 2), 7 - me)
    for part, ref in enumerate(kv_refs):
        owner, index, parts = starts[part]
        place = (row + (owners[owner] * parts + index) * rows).astype(f32)
        bias = jnp.where(place < live, 0.0, DEAD)
        kaug[part * rows : part * rows + rows, :HD] = ref[:, :HD]
        kaug[part * rows : part * rows + rows, HD:] = jnp.where(lane == 6, bias, ones).astype(bf16)


def forward_kernel(ctx, counts, *refs, blocks, starts, first, last):
    refs = list(refs)

    def take(count):
        taken = refs[:count]
        del refs[:count]
        return taken

    pieces = len(starts)
    if first:
        q_refs = take(blocks)
    else:
        (q_all,) = take(1)
    kv_refs = take(pieces)
    if not first:
        acc_in, stat_in = take(2)
    if last:
        out_refs = take(blocks)
    else:
        acc_out, stat_out = take(2)
    if first:
        (q_all,) = take(1)
    kaug, v_t, *scores = take(4)
    if last:
        (out_all,) = take(1)
    rows = kv_refs[0].shape[0]
    keys = pieces * rows
    wide = q_all.shape[2]
    fill_keys(ctx, counts, starts, kv_refs, kaug)
    for part, ref in enumerate(kv_refs):
        v_t[:, part * rows : part * rows + rows] = ref[:, HD:].astype(f32).T.astype(bf16)
    if first:
        sub = lax.broadcasted_iota(jnp.int32, (HD, wide), 0)
        tail = jnp.where(sub == 6, 1.0, 0.0).astype(bf16)
        for i in range(blocks):
            q_all[i, :HD, :] = q_refs[i][...]
            q_all[i, HD:, :] = tail
    spans = [slice(j * CHUNK, j * CHUNK + CHUNK) for j in range(keys // CHUNK)]

    def score(i, slot, span, top):
        s = dot(kaug[span, :], q_all[i], NN)
        scores[slot][span, :] = s
        return jnp.maximum(top, jnp.max(s, axis=0, keepdims=True))

    def start(i):
        return jnp.full((1, wide), -jnp.inf, f32) if first else stat_in[i, 0:1, :]

    def block(i, slot, top, follow):
        if first:
            total = jnp.zeros((1, wide), f32)
            acc = jnp.zeros((HD, wide), f32)
        else:
            shrink = jnp.exp2((stat_in[i, 0:1, :] - top) * EXP2_SCALE)
            total = stat_in[i, 1:2, :] * shrink
            acc = acc_in[i] * shrink
        following = start(follow)
        for span in spans:
            following = score(follow, 1 - slot, span, following)
            p = jnp.exp2((scores[slot][span, :] - top) * EXP2_SCALE)
            total = total + jnp.sum(p, axis=0, keepdims=True)
            acc = acc + dot(v_t[:, span], p.astype(bf16), NN)
        if not last:
            acc_out[i] = acc
            which = lax.broadcasted_iota(jnp.int32, (8, wide), 0)
            stat_out[i] = jnp.where(which == 0, top, total)
        else:
            out_all[i, :HD, :] = (acc / total).astype(bf16)
            high, middle, low = split3(top + jnp.log(total) * (1.0 / SCALE))
            which = lax.broadcasted_iota(jnp.int32, (EXTRA, wide), 0)
            rest = jnp.where(which == 1, middle, jnp.where(which == 2, low, 0.0))
            out_all[i, HD:, :] = jnp.where(which == 0, high, rest).astype(bf16)
        return following

    top = start(0)
    for span in spans:
        top = score(0, 0, span, top)

    def pair(t, top):
        middle = block(2 * t, 0, top, 2 * t + 1)
        return block(2 * t + 1, 1, middle, jnp.minimum(2 * t + 2, blocks - 1))

    lax.fori_loop(0, blocks // 2, pair, top)
    if last:
        for i in range(blocks):
            out_refs[i][...] = out_all[i]


def forward(ctx, counts, q_blocks, kv_pieces, starts, before=(), last=False):
    first = not before
    blocks, wide = (len(q_blocks), q_blocks[0].shape[1]) if first else q_blocks.shape[::2]
    keys = len(kv_pieces) * kv_pieces[0].shape[0]
    if last:
        outs = [((HD + EXTRA, wide), bf16)] * blocks
    else:
        outs = [((blocks, HD, wide), f32), ((blocks, 8, wide), f32)]
    if first:
        outs.append(((blocks, 2 * HD, wide), bf16))
    args = [*(q_blocks if first else [q_blocks]), *kv_pieces, *before]
    return call(
        functools.partial(forward_kernel, blocks=blocks, starts=starts, first=first, last=last),
        [SMEM] + [VMEM] * (len(args) + 1),
        outs,
        [
            pltpu.VMEM((keys, 2 * HD), bf16),
            pltpu.VMEM((HD, keys), bf16),
            pltpu.VMEM((keys, wide), f32),
            pltpu.VMEM((keys, wide), f32),
        ]
        + ([pltpu.VMEM((blocks, HD + EXTRA, wide), bf16)] if last else []),
        work=10**10,
        limit=13 if first else 8,
    )(ctx, counts, *args)


def one_hot(place):
    rows = place.shape[1]
    row = lax.broadcasted_iota(jnp.int32, (rows, rows), 0)
    return jnp.where(row == place[...], 1.0, 0.0).astype(bf16)


def combine_kernel(ctx, place, *refs):
    partial, (out_t, logs, c0, c1, c2, c3) = refs[:4], refs[4:]
    wide = partial[0].shape[1]
    for side in range(2):
        sums = []
        for ref in partial[2 * side : 2 * side + 2]:
            tail = ref[HD:, :].astype(f32)
            sums.append(tail[0:1] + tail[1:2] + tail[2:3])
        top = functools.reduce(jnp.maximum, sums)
        weight = [jnp.exp2((s - top) * EXP2_SCALE) for s in sums]
        total = sum(weight)
        acc = jnp.zeros((HD, wide), f32)
        for w, ref in zip(weight, partial[2 * side : 2 * side + 2]):
            acc = acc + (w / total) * ref[:HD, :].astype(f32)
        logs[side, :, :] = jnp.broadcast_to(top + jnp.log(total) * (1.0 / SCALE), (8, wide))
        head = ctx[0] % 2 if side == 0 else 1 - ctx[0] % 2
        out_t[pl.ds(pl.multiple_of(head * HD, HD), HD), :] = acc.astype(bf16)
    grouped = dot(one_hot(place), out_t[...], NT).astype(bf16)
    quarter = wide // 4
    for i, ref in enumerate((c0, c1, c2, c3)):
        ref[...] = grouped[i * quarter : i * quarter + quarter]


def project_kernel(o0, o1, o2, o3, w0, w1, w2, w3, x0, x1, x2, x3):
    total = None
    for o, w in ((o0, w0), (o1, w1), (o2, w2), (o3, w3)):
        term = dot(o[...], w[...], NN)
        total = term if total is None else total + term
    rows = x0.shape[0]
    for i, ref in enumerate((x0, x1, x2, x3)):
        ref[...] = total[i * rows : i * rows + rows].astype(ref.dtype)


def unproject_kernel(g0, g1, g2, g3, w0, w1, w2, w3, d0, d1, d2, d3, g):
    rows = g0.shape[0]
    for i, ref in enumerate((g0, g1, g2, g3)):
        g[i * rows : i * rows + rows, :] = ref[...]
    for w, d in ((w0, d0), (w1, d1), (w2, d2), (w3, d3)):
        d[...] = dot(g[...], w[...], NT).astype(bf16)


def center(x):
    mean = jnp.mean(x, axis=1, keepdims=True)
    shifted = x - mean
    rate = lax.rsqrt(jnp.mean(shifted * shifted, axis=1, keepdims=True) + EPSILON)
    return shifted * rate, rate


def center_grad(grad, normed, rate):
    return rate * (
        grad
        - jnp.mean(grad, axis=1, keepdims=True)
        - normed * jnp.mean(grad * normed, axis=1, keepdims=True)
    )


def reward_kernel(counts, x0, x1, x2, x3, head, up, down, grad_out, reward_out, slopes):
    steps, _, part = slopes.shape
    vision = up.shape[0]

    def piece(j):
        return pl.ds(pl.multiple_of(j * part, part), part)

    rows = x0.shape[0]

    def live(shape, axis):
        row = lax.broadcasted_iota(jnp.int32, shape, axis)
        left = jnp.where(row < FTOK, counts[0], counts[1] + FTOK)
        return jnp.where(row < left, 1.0, 0.0)

    x = x0[...].astype(f32) + x1[...].astype(f32) + x2[...].astype(f32) + x3[...].astype(f32)
    normed, rate = center(x)
    low_normed = normed.astype(bf16)
    c0 = math.sqrt(2.0 / math.pi)
    c1 = 0.044715

    def upward(j, hidden):
        before = dot(low_normed, up[:, piece(j)], NN)
        square = before * before
        tanh = jnp.tanh(c0 * before * (1.0 + c1 * square))
        half = 0.5 * (1.0 + tanh)
        slope = half + 0.5 * before * (1.0 - tanh * tanh) * (c0 * (1.0 + 3.0 * c1 * square))
        slopes[j] = slope
        return hidden + dot((before * half).astype(bf16), down[piece(j), :], NN)

    hidden = lax.fori_loop(0, steps, upward, jnp.zeros((rows, vision), f32))
    alive = live((rows, 1), 0)
    count = jnp.sum(alive, axis=0, keepdims=True)
    pooled = jnp.sum(hidden * alive, axis=0, keepdims=True) / count
    pooled_normed, pooled_rate = center(pooled)
    reward = count * jnp.sum(pooled_normed * head[...], axis=1, keepdims=True)
    reward_out[...] = jnp.broadcast_to(reward, reward_out.shape)
    pooled_grad = center_grad(count * head[...], pooled_normed, pooled_rate) / count
    high, middle, low = split3(pooled_grad)
    which = lax.broadcasted_iota(jnp.int32, (EXTRA, vision), 0)
    pieces = jnp.where(which == 0, high, jnp.where(which == 1, middle, jnp.where(which == 2, low, 0.0)))
    pieces_b = pieces.astype(bf16)
    alive_t = live((1, rows), 1)

    def downward(j, normed_grad):
        spread = jnp.sum(dot(pieces_b, down[piece(j), :], NT), axis=0, keepdims=True)
        before_grad = (spread * slopes[j] * alive).astype(bf16)
        return normed_grad + dot(before_grad, up[:, piece(j)], NT)

    normed_grad = lax.fori_loop(0, steps, downward, jnp.zeros((rows, vision), f32))
    grad_out[...] = center_grad(normed_grad, normed, rate).astype(bf16)


def reward_call(counts, inputs, head, mlp_up, mlp_down):
    vision, hidden = mlp_up.shape
    steps = 8
    part = hidden // steps
    rows = inputs[0].shape[0]
    return call(
        reward_kernel,
        [SMEM] + [VMEM] * 7,
        [((rows, vision), bf16), ((8, HD), f32)],
        [
            pltpu.VMEM((steps, rows, part), f32),
        ],
    )(counts, *inputs, head.reshape(1, -1), mlp_up, mlp_down)


def ungroup_kernel(ctx, place, d0, d1, d2, d3, out_t, logs, ps, po, grad):
    quarter = d0.shape[0]
    for i, ref in enumerate((d0, d1, d2, d3)):
        grad[i * quarter : i * quarter + quarter, :] = ref[...]
    wide = place.shape[1]
    grad_t = dot(grad[...], one_hot(place), TN)
    product = grad_t * out_t[...].astype(f32)
    which = lax.broadcasted_iota(jnp.int32, (EXTRA, wide), 0)
    for head in range(2):
        delta = jnp.sum(product[head * HD : head * HD + HD], axis=0, keepdims=True)
        for side, ref in enumerate((ps, po)):

            @pl.when(head == (ctx[0] % 2 if side == 0 else 1 - ctx[0] % 2))
            def _():
                ref[:HD, :] = grad_t[head * HD : head * HD + HD].astype(bf16)
                rows = split3(delta) + split3(-logs[side, 0:1, :])
                tail = jnp.where(which == 6, 1.0, 0.0)
                for i, piece in enumerate(rows):
                    tail = jnp.where(which == i, piece, tail)
                ref[HD:, :] = tail.astype(bf16)


def backward_kernel(ctx, counts, *refs, blocks, starts, first, last):
    refs = list(refs)

    def take(count):
        taken = refs[:count]
        del refs[:count]
        return taken

    pieces = len(starts)
    (q_in,) = take(1)
    g_refs = take(blocks)
    kv_refs = take(pieces)
    if not first:
        (dq_in,) = take(1)
    dq_refs = take(blocks) if last else take(1)
    out_refs = take(2) if last else take(1)
    kaug, vaug, k_t, q_all, g_all, dk, dv = take(7)
    if last:
        (dq_all,) = take(1)
    rows = kv_refs[0].shape[0]
    keys = pieces * rows
    wide = q_in.shape[2]
    fill_keys(ctx, counts, starts, kv_refs, kaug)
    lane = lax.broadcasted_iota(jnp.int32, (rows, HD), 1)
    minus = jnp.where(lane < 3, -1.0, 0.0).astype(bf16)
    for part, ref in enumerate(kv_refs):
        where = slice(part * rows, part * rows + rows)
        vaug[where, :HD] = ref[:, HD:]
        vaug[where, HD:] = minus
        k_t[:, where] = ref[:, :HD].astype(f32).T.astype(bf16)
    dk[...] = jnp.zeros_like(dk)
    dv[...] = jnp.zeros_like(dv)
    blank = jnp.zeros((HD - EXTRA, wide), bf16)
    for i in range(blocks):
        q_all[i, :HD, :] = q_in[i, :HD, :]
        q_all[i, HD : HD + EXTRA, :] = g_refs[i][HD:, :]
        q_all[i, HD + EXTRA :, :] = blank
        g_all[i, : HD + EXTRA, :] = g_refs[i][...]
        g_all[i, HD + EXTRA :, :] = blank

    def block(i, carry):
        query = q_all[i]
        grad = g_all[i]
        acc = jnp.zeros((HD, wide), f32) if first else dq_in[i]
        for j in range(keys // CHUNK):
            part = slice(j * CHUNK, j * CHUNK + CHUNK)
            p = jnp.exp2(dot(kaug[part, :], query, NN) * EXP2_SCALE)
            ds = (p * dot(vaug[part, :], grad, NN)).astype(bf16)
            dv[part, :] += dot(p.astype(bf16), grad[:HD], NT)
            dk[part, :] += dot(ds, query[:HD], NT)
            acc = acc + dot(k_t[:, part], ds, NN)
        if last:
            dq_all[i] = (acc * SCALE).astype(bf16)
        else:
            dq_refs[0][i] = acc
        return carry

    lax.fori_loop(0, blocks, block, 0)
    if last:
        for i in range(blocks):
            dq_refs[i][...] = dq_all[i]
    if last:
        out_refs[0][...] = dk[...] * SCALE
        out_refs[1][...] = dv[...]
    else:
        out_refs[0][:, :HD] = (dk[...] * SCALE).astype(bf16)
        out_refs[0][:, HD:] = dv[...].astype(bf16)


def backward(ctx, counts, q_blocks, g_blocks, kv_pieces, starts, before=None, last=False):
    blocks, _, wide = q_blocks.shape
    pieces = len(kv_pieces)
    rows = kv_pieces[0].shape[0]
    keys = pieces * rows
    if last:
        outs = [((HD, wide), bf16)] * blocks + [((keys, HD), f32)] * 2
    else:
        outs = [((blocks, HD, wide), f32), ((keys, 2 * HD), bf16)]
    scratch = [
        pltpu.VMEM((keys, 2 * HD), bf16),
        pltpu.VMEM((keys, 2 * HD), bf16),
        pltpu.VMEM((HD, keys), bf16),
        pltpu.VMEM((blocks, 2 * HD, wide), bf16),
        pltpu.VMEM((blocks, 2 * HD, wide), bf16),
        pltpu.VMEM((keys, HD), f32),
        pltpu.VMEM((keys, HD), f32),
    ]
    if last:
        scratch.append(pltpu.VMEM((blocks, HD, wide), bf16))
    args = [q_blocks, *g_blocks, *kv_pieces] + ([] if before is None else [before])
    out = call(
        functools.partial(
            backward_kernel, blocks=blocks, starts=starts, first=before is None, last=last
        ),
        [SMEM] + [VMEM] * (len(args) + 1),
        outs,
        scratch,
        work=2 * 10**10,
    )(ctx, counts, *args)
    count = blocks if last else 1
    return (out[:blocks] if last else out[0]), out[count:]


def unrotate(x, c, s):
    return x * c - pltpu.roll(x, HD // 2, 1) * s


def query_grad_kernel(ctx, table, d0, d1, d2, d3, out):
    c, s = spread_angles(table)
    for which in range(2):

        @pl.when(ctx[0] % 2 == which)
        def _():
            for head, one, two in ((which, d0, d1), (1 - which, d2, d3)):
                total = one[...].astype(f32) + two[...].astype(f32)
                out[:, head * HD : head * HD + HD] = unrotate(total.T, c, s)


def key_grad_kernel(ctx, table, dk, dv, far, par, far_par, dk_out, dv_out):
    c, s = spread_angles(table)
    for which in range(2):

        @pl.when(ctx[0] % 2 == which)
        def _():
            cols = slice(which * HD, which * HD + HD)
            dk_out[:, cols] = unrotate(dk[...] + far[:, :HD].astype(f32), c, s)
            dv_out[:, cols] = dv[...] + far[:, HD:].astype(f32)
            cols = slice(HD - which * HD, 2 * HD - which * HD)
            total = par[...].astype(f32) + far_par[...].astype(f32)
            dk_out[:, cols] = unrotate(total[:, :HD], c, s)
            dv_out[:, cols] = total[:, HD:]


def ctx_swap(turn, flip):
    def target(x, z):
        x = (x, x ^ 1, 3 - x)[turn]
        return x * 2 + (z ^ flip)

    return [(x * 2 + z, target(x, z)) for x in range(4) for z in range(2)]


def send_ctx(array, turn, flip):
    return lax.ppermute(array, "ctx", ctx_swap(turn, flip))


def frame_xor(mask):
    return [(i, i ^ mask) for i in range(16)]


QUAD_MASKS = (0, 1, 8, 9)
Y_MASKS = (0, 2, 4, 6)


def send_frame(array, mask):
    return array if mask == 0 else lax.ppermute(array, "frame", frame_xor(mask))


def exchange(blocks):
    same, near, other, near_other = blocks
    return [same, send_ctx(near, 1, 0), send_ctx(other, 0, 1), send_ctx(near_other, 1, 1)]


def shards(
    queries,
    keys,
    values,
    query_frames,
    frame_counts,
    clip_of_frame,
    in_proj,
    mlp_up,
    mlp_down,
    reward_head,
):
    ctx_index = lax.axis_index("ctx")
    frame_index = lax.axis_index("frame")
    query_rows = queries.shape[0]
    key_rows = keys.shape[0]
    frame_slots = query_frames.shape[0]
    key_frames = frame_counts.shape[0]
    in_frame = jnp.arange(FTOK, dtype=jnp.int32)
    ctx = ctx_index.reshape(1).astype(jnp.int32)
    counts = frame_counts.reshape(-1, HD)
    packed_rows = ((key_rows, 2 * HD), bf16)
    any_space = pl.BlockSpec(memory_space=pltpu.HBM)
    high_rows = key_rows // 2
    kv_own, kv_send, kv_high, key_table, qs, qo, query_table = call(
        rotate_kernel,
        [SMEM] + [any_space] * 4,
        [packed_rows] * 2
        + [((high_rows, 2 * HD), bf16), ((2, key_rows // FTOK + FTOK, HD), f32)]
        + [((HD, query_rows), bf16)] * 2
        + [((2, frame_slots + FTOK, HD), f32)],
        [
            pltpu.VMEM(queries.shape, bf16),
            pltpu.VMEM(keys.shape, bf16),
            pltpu.VMEM(values.shape, bf16),
            pltpu.SMEM((frame_slots,), jnp.int32),
            pltpu.VMEM((frame_slots, HD), f32),
            pltpu.SemaphoreType.DMA((4,)),
        ],
    )(ctx, query_frames, queries, keys, values)
    kv_far = send_ctx(kv_own, 2, 0)
    q_blocks = exchange((qs, qs, qo, qo))
    kv_par = send_ctx(kv_send, 0, 1)

    slot_index = jnp.arange(frame_slots, dtype=jnp.int32)
    same_clip = clip_of_frame[:, None] == clip_of_frame[None, :]
    earlier = slot_index[None, :] < slot_index[:, None]
    rank = jnp.sum(jnp.logical_and(same_clip, earlier), axis=1).astype(jnp.int32)
    away = clip_of_frame ^ frame_index
    quad = (away >> 3) * 2 + (away & 1)
    slot_place = (quad * 4 + ((away >> 1) & 3)) * CLIP + rank
    place = (slot_place[:, None] * FTOK + in_frame[None, :]).reshape(1, query_rows)
    frame_match = query_frames[:, None] == jnp.arange(key_frames, dtype=jnp.int32)[None, :]
    slot_counts = jnp.sum(jnp.where(frame_match, frame_counts[None, :], 0), axis=1)
    mine = slot_place[None, :] == jnp.arange(CLIP, dtype=jnp.int32)[:, None]
    my_counts = jnp.sum(jnp.where(mine, slot_counts[None, :], 0), axis=1).astype(jnp.int32)

    kv_far_high = send_ctx(kv_high, 2, 1)
    *state, q_blocks = forward(
        ctx, counts, q_blocks, (kv_own, kv_far), ((0, 0, 1), (2, 0, 1))
    )
    kv_par, _ = lax.optimization_barrier((kv_par, state[1]))
    kv_far_low = send_ctx(kv_par[:high_rows], 2, 0)
    state = forward(ctx, counts, q_blocks, (kv_par,), ((1, 0, 1),), state)
    in_proj, _ = lax.optimization_barrier((in_proj, state[1]))
    near = send_frame(in_proj, 8)
    kv_far_par = (kv_far_low, kv_far_high)
    far_par = ((3, 0, 2), (3, 1, 2))
    partial = forward(ctx, counts, q_blocks, kv_far_par, far_par, state, True)
    in_proj, near_late, _ = lax.optimization_barrier((in_proj, near, partial[0]))
    weights = (in_proj, send_frame(in_proj, 1), near_late, send_frame(near_late, 1))
    partial = exchange(partial)
    width = queries.shape[1]
    quarter = query_rows // 4
    out_t, logs, *chunks = call(
        combine_kernel,
        [SMEM] + [VMEM] * 5,
        [((width, query_rows), bf16), ((2, 8, query_rows), f32)] + [((quarter, width), bf16)] * 4,
        work=5 * 10**9,
    )(ctx, place, *partial)
    chunks = [send_frame(chunk, mask) for chunk, mask in zip(chunks, QUAD_MASKS)]
    vision = in_proj.shape[1]
    clip_rows = CLIP * FTOK
    inputs = call(
        project_kernel,
        [VMEM] * 8,
        [((clip_rows, vision), f32)] + [((clip_rows, vision), bf16)] * 3,
        work=5 * 10**9,
    )(*chunks, *weights)
    inputs = [send_frame(x, mask) for x, mask in zip(inputs, Y_MASKS)]
    input_grad, reward = reward_call(my_counts, inputs, reward_head, mlp_up, mlp_down)
    grads = [send_frame(input_grad, mask) for mask in Y_MASKS]
    grads = call(
        unproject_kernel,
        [VMEM] * 8,
        [((quarter, width), bf16)] * 4,
        [pltpu.VMEM((quarter, vision), bf16)],
    )(*grads, *weights)
    grads = [send_frame(grad, mask) for grad, mask in zip(grads, QUAD_MASKS)]
    packed = (HD + EXTRA, query_rows)
    gs, go = call(
        ungroup_kernel,
        [SMEM] + [VMEM] * 7,
        [(packed, bf16)] * 2,
        [pltpu.VMEM((query_rows, width), bf16)],
    )(ctx, place, *grads, out_t, logs)
    g_blocks = exchange((gs, gs, go, go))
    dq, (d_far_par,) = backward(ctx, counts, q_blocks, g_blocks, kv_far_par, far_par)
    d_far_par = send_ctx(d_far_par, 2, 1)
    dq, (d_par,) = backward(ctx, counts, q_blocks, g_blocks, (kv_par,), ((1, 0, 1),), dq)
    d_par = send_ctx(d_par, 0, 1)
    dq, (d_far,) = backward(ctx, counts, q_blocks, g_blocks, (kv_far,), ((2, 0, 1),), dq)
    d_far = send_ctx(d_far, 2, 0)
    dq, (dk_own, dv_own) = backward(
        ctx, counts, q_blocks, g_blocks, (kv_own,), ((0, 0, 1),), dq, True
    )
    dq = exchange(dq)
    (query_grad,) = call(
        query_grad_kernel,
        [SMEM] + [VMEM] * 5,
        [((query_rows, width), f32)],
    )(ctx, query_table, *dq)
    key_grad, value_grad = call(
        key_grad_kernel,
        [SMEM] + [VMEM] * 6,
        [((key_rows, width), f32)] * 2,
    )(ctx, key_table, dk_own, dv_own, d_far, d_par, d_far_par)
    return query_grad, key_grad, value_grad, reward[0, :1]


def solution(mesh):
    return jax.shard_map(
        shards,
        mesh=mesh,
        in_specs=(
            P("ctx", "frame"),
            P("ctx", "frame"),
            P("ctx", "frame"),
            P("ctx"),
            P(),
            P("ctx"),
            P("frame", None),
            P(),
            P(),
            P(),
        ),
        out_specs=(P("ctx", "frame"), P("ctx", "frame"), P("ctx", "frame"), P(("ctx", "frame"))),
        check_vma=False,
    )
```
